32 devices in a mesh: ma: 4 (over y, core), row: 8 (over z, x).
Axes of the slice: x: 2, y: 2, z: 4, core: 2. Of those that a mesh axis runs over, the one named last changes fastest.
Arguments:
- grid_fields: bfloat16 [4, 16, 1536, 2048], P(None, 'row', 'ma'), may hold values from -6 to 6
- pair_list: int32 [256], replicated, may hold values from 0 to 255, each once
- legendre: bfloat16 [256, 768, 1024], P(('ma', 'row')), may hold values from -0.21875 to 0.21875
- stencil_start: int32 [16], replicated, may hold values from 0 to 11, as said below
- first_weights: float32 [16, 5], replicated, may hold values from -6 to 6
- second_weights: float32 [16, 5], replicated, may hold values from -6 to 6
- inv_radius: float32 [16], replicated, may hold values from 1 to 2.86
Outputs:
- current: bfloat16 [3, 2, 256, 16, 1024], P(None, None, ('ma', 'row'))
- vorticity: bfloat16 [3, 2, 256, 16, 1024], P(None, None, ('ma', 'row'))
The draws below stay inside these ranges and needn't reach their ends.
Inputs may be any that keep to these rules, and one draw needn't show every extreme that they name: Every radius r lies inside its own stencil: stencil_start[r] <= r <= stencil_start[r] + 4.
All inputs are finite; a program needn't handle non-finite values.
Results may differ from the reference program's by a relative error of at most 0.0072.
Values may be sent and summed in bfloat16 or wider, within the bound.
A program may use at most 192 MiB of HBM per device.

```python
import math
import jax
import jax.numpy as jnp
from jax import lax

L = 1024
NLAT = 1536
NLON = 2048
PAIRS = 256
POT = 4
STEN = 5
R = 16


def draw_stencil_start(key, part):
    offsets = jax.random.randint(key, (R,), 0, STEN)
    return jnp.clip(jnp.arange(R) - offsets, 0, R - STEN).astype(jnp.int32)


def shard_levels(own_key, dims, pieces, low, top_value):
    def one(dim, blocks):
        draws = jax.random.uniform(jax.random.fold_in(jax.random.fold_in(own_key, 6), dim), (blocks,), jnp.float32, low / len(pieces), top_value / len(pieces))
        return jnp.repeat(jnp.exp(draws), dims[dim] // blocks).reshape((-1,) + (1,) * (len(dims) - dim - 1))

    loudness = one(*pieces[0])
    for cut in pieces[1:]:
        loudness = loudness * one(*cut)
    return loudness


def scatter_about(key, dims, deviation, limit, shards=(), held_as=jnp.bfloat16):
    result = deviation * jax.random.normal(key, dims, jnp.float32)
    if shards:
        result = result * shard_levels(key, dims, shards, -0.22, 0.18)
    return jnp.clip(result, -limit, limit).astype(held_as)


def setup_inputs(seed: int = 0) -> dict:
    keys = jax.random.split(jax.random.key(seed), 8)
    grid_fields = scatter_about(keys[0], (POT, R, NLAT, NLON), 1.0, 6.0, ((1, 8), (2, 4)))
    pair_list = jax.random.permutation(keys[1], PAIRS).astype(jnp.int32)
    legendre = scatter_about(keys[2], (PAIRS, NLAT // 2, L), (NLAT // 2) ** -0.5, 0.21875, ((0, 32),))
    stencil_start = draw_stencil_start(jax.random.fold_in(keys[7], 71), 0)
    first_weights = scatter_about(keys[4], (R, STEN), 1.0, 6.0, (), jnp.float32)
    second_weights = scatter_about(keys[5], (R, STEN), 1.0, 6.0, (), jnp.float32)
    inv_radius = jnp.clip(jnp.exp(jax.random.uniform(keys[6], (R,), jnp.float32, math.log(1.0), math.log(2.86))), 1.0, 2.86)
    return {"grid_fields": grid_fields, "pair_list": pair_list, "legendre": legendre, "stencil_start": stencil_start, "first_weights": first_weights, "second_weights": second_weights, "inv_radius": inv_radius}


def degree_table(pair_values, degrees):
    column = jnp.arange(degrees, dtype=jnp.int32)
    upper_side = column[None, :] >= (degrees - pair_values)[:, None]
    degree = jnp.where(upper_side, column[None, :], pair_values[:, None] + column[None, :])
    order_value = jnp.where(upper_side, degrees - pair_values[:, None], pair_values[:, None])
    parity = (degree - order_value) % 2
    return (upper_side.astype(jnp.int32), parity, degree)

def fourier_table(pair_values, degrees, points):
    orders = jnp.stack([pair_values, degrees - pair_values], axis=1)
    longitude = jnp.arange(points, dtype=jnp.int32)
    phases = orders[None, :, :] * longitude[:, None, None] % points
    angles = phases.astype(jnp.float32) * (2.0 * math.pi / points)
    factor = 1.0 / math.sqrt(points)
    return jnp.stack([jnp.cos(angles) * factor, -jnp.sin(angles) * factor], axis=-1).astype(jnp.bfloat16)

def derivative_matrix(stencil_start, weights):
    radius_count, stencil_width = weights.shape
    target = stencil_start[:, None] + jnp.arange(stencil_width, dtype=jnp.int32)[None, :]
    matches = target[:, :, None] == jnp.arange(radius_count, dtype=jnp.int32)[None, None, :]
    return lax.optimization_barrier(jnp.sum(jnp.where(matches, weights[:, :, None], 0.0), axis=1))

def radial(matrix, values):
    return jnp.einsum('rt,cjtk->cjrk', matrix, values, precision=lax.Precision.HIGHEST)

def curl_parts(poloidal, toroidal, first_matrix, second_matrix, horizontal, inverse):
    poloidal_first = radial(first_matrix, poloidal)
    poloidal_second = radial(second_matrix, poloidal)
    toroidal_first = radial(first_matrix, toroidal)
    radial_part = horizontal * inverse * toroidal
    spheroidal = toroidal_first + inverse * toroidal
    toroidal_part = -(poloidal_second + 2.0 * inverse * poloidal_first) + horizontal * inverse * inverse * poloidal
    return jnp.stack([radial_part, spheroidal, toroidal_part], axis=0).astype(jnp.bfloat16)

def reference(grid_fields, pair_list, legendre, stencil_start, first_weights, second_weights, inv_radius):
    fourier = fourier_table(pair_list, L, NLON).reshape(NLON, PAIRS * 4)

    def analyse(radius_index):
        one_radius = lax.dynamic_index_in_dim(grid_fields, radius_index, 1, False)
        flat = one_radius.reshape(POT * NLAT, NLON)
        values = jnp.dot(flat, fourier, preferred_element_type=jnp.float32)
        return values.astype(jnp.bfloat16).reshape(POT, NLAT, PAIRS, 2, 2)
    coefficients = lax.map(analyse, jnp.arange(R, dtype=jnp.int32))
    upper_side, parity, degree = degree_table(pair_list, L)
    two_values = jnp.arange(2, dtype=jnp.int32)

    def per_slot(slot_index):
        portion = lax.dynamic_index_in_dim(coefficients, slot_index, 3, False).astype(jnp.float32)
        northern = portion[:, :, :NLAT // 2]
        southern = jnp.flip(portion[:, :, NLAT // 2:], axis=2)
        folded = jnp.stack([northern + southern, northern - southern], axis=0).astype(jnp.bfloat16)
        matrix_block = jnp.moveaxis(folded, 3, 0).reshape(NLAT // 2, 2 * R * POT * 4)
        table_rows = lax.dynamic_index_in_dim(legendre, slot_index, 0, False)
        product = jnp.dot(matrix_block.T, table_rows, preferred_element_type=jnp.float32)
        product = product.reshape(2, R, POT, 2, 2, L)
        slot_parity = lax.dynamic_index_in_dim(parity, slot_index, 0, False)
        slot_side = lax.dynamic_index_in_dim(upper_side, slot_index, 0, False)
        selector = ((slot_parity[None, None, :] == two_values[:, None, None]) & (slot_side[None, None, :] == two_values[None, :, None])).astype(jnp.float32)
        chosen = lax.optimization_barrier(jnp.sum(product * selector[:, None, None, :, None, :], axis=(0, 3)))
        return jnp.transpose(chosen, (1, 2, 0, 3)).astype(jnp.bfloat16)
    spectral = jnp.transpose(lax.map(per_slot, jnp.arange(PAIRS, dtype=jnp.int32)), (1, 2, 0, 3, 4))
    first_matrix = derivative_matrix(stencil_start, first_weights)
    second_matrix = derivative_matrix(stencil_start, second_weights)
    horizontal = ((degree * (degree + 1)).astype(jnp.float32) / (L * L))[None, :, None, :]
    inverse = inv_radius[:, None]
    current = curl_parts(spectral[0].astype(jnp.float32), spectral[1].astype(jnp.float32), first_matrix, second_matrix, horizontal, inverse)
    vorticity = curl_parts(spectral[2].astype(jnp.float32), spectral[3].astype(jnp.float32), first_matrix, second_matrix, horizontal, inverse)
    return (current, vorticity)
```

```python
import functools
import math

import jax
import jax.numpy as jnp
import ml_dtypes
import numpy as np
from jax import lax
from jax.experimental import pallas as pl
from jax.experimental.pallas import tpu as pltpu
from jax.sharding import PartitionSpec as P

MESH = pl.DeviceIdType.MESH
F32 = jnp.float32
BF16 = jnp.bfloat16


def degree_table(pair_values, degrees):
    column = jnp.arange(degrees, dtype=jnp.int32)
    upper_side = column[None, :] >= (degrees - pair_values)[:, None]
    degree = jnp.where(upper_side, column[None, :], pair_values[:, None] + column[None, :])
    order_value = jnp.where(upper_side, degrees - pair_values[:, None], pair_values[:, None])
    parity = (degree - order_value) % 2
    return (upper_side.astype(jnp.int32), parity, degree)


def derivative_matrix(stencil_start, weights):
    radius_count, stencil_width = weights.shape
    target = stencil_start[:, None] + jnp.arange(stencil_width, dtype=jnp.int32)[None, :]
    matches = target[:, :, None] == jnp.arange(radius_count, dtype=jnp.int32)[None, None, :]
    return jnp.sum(jnp.where(matches, weights[:, :, None], 0.0), axis=1)


def fourier_table(pair_values, degrees, points):
    orders = jnp.stack([pair_values, degrees - pair_values], axis=1)
    stride = 128
    factor = 1.0 / math.sqrt(points)

    def waves(positions):
        phases = orders[:, :, None] * positions[None, None, :] % points
        angles = phases.astype(jnp.float32) * (2.0 * math.pi / points)
        return jnp.cos(angles), jnp.sin(angles)

    wide_cos, wide_sin = waves(jnp.arange(points // stride, dtype=jnp.int32) * stride)
    fine_cos, fine_sin = waves(jnp.arange(stride, dtype=jnp.int32))
    wide_cos, wide_sin = wide_cos[..., None] * factor, wide_sin[..., None] * factor
    fine_cos, fine_sin = fine_cos[:, :, None, :], fine_sin[:, :, None, :]
    cosine = wide_cos * fine_cos - wide_sin * fine_sin
    sine = wide_sin * fine_cos + wide_cos * fine_sin
    table = jnp.stack([cosine, -sine], axis=2).astype(jnp.bfloat16)
    return table.reshape(pair_values.shape[0], 4, points)


def radial(matrix, values):
    return jnp.einsum("rt,cjtk->cjrk", matrix, values, precision=lax.Precision.HIGHEST)


def curl_parts(poloidal, toroidal, first_matrix, second_matrix, horizontal, inverse):
    poloidal_first = radial(first_matrix, poloidal)
    poloidal_second = radial(second_matrix, poloidal)
    toroidal_first = radial(first_matrix, toroidal)
    radial_part = horizontal * inverse * toroidal
    spheroidal = toroidal_first + inverse * toroidal
    toroidal_part = (
        -(poloidal_second + 2.0 * inverse * poloidal_first)
        + horizontal * inverse * inverse * poloidal
    )
    return jnp.stack([radial_part, spheroidal, toroidal_part], axis=0).astype(jnp.bfloat16)


def select_columns(product, pair_values, degrees):
    upper_side, parity, _ = degree_table(pair_values, degrees)
    wide = (slice(None),) + (None,) * 3 + (slice(None),)
    by_side = jnp.where(upper_side[:, None][wide] == 1, product[:, :, 1], product[:, :, 0])
    return jnp.where(parity[wide] == 1, by_side[:, 1], by_side[:, 0])


def plain_shards(
    grid_fields, pair_list, legendre, stencil_start, first_weights, second_weights, inv_radius
):
    potentials, rad_local, lat_local, points = grid_fields.shape
    degrees = legendre.shape[2]
    slots_here = legendre.shape[0]
    band_count = lax.axis_size("ma")
    rows_axis = lax.axis_size("row")
    fourier = fourier_table(pair_list, degrees, points)
    coefficients = jnp.einsum(
        "jsx,prhx->jsprh", fourier, grid_fields, preferred_element_type=jnp.float32
    ).astype(jnp.bfloat16)
    southern = lax.axis_index("ma") >= band_count // 2
    coefficients = jnp.where(southern, jnp.flip(coefficients, axis=-1), coefficients)
    at_owners = lax.all_to_all(
        coefficients, ("ma", "row"), split_axis=0, concat_axis=0, tiled=True
    ).reshape(band_count, rows_axis, slots_here, 2, 2, potentials, rad_local, lat_local)
    first_slot = (lax.axis_index("ma") * rows_axis + lax.axis_index("row")) * slots_here
    own_pairs = lax.dynamic_slice_in_dim(pair_list, first_slot, slots_here, 0)
    widened = at_owners.astype(jnp.float32)
    north = widened[: band_count // 2]
    south = jnp.flip(widened[band_count // 2 :], axis=0)
    folded = jnp.stack([north + south, north - south], axis=0).astype(jnp.bfloat16)
    folded = jnp.transpose(folded, (3, 0, 4, 5, 6, 2, 7, 1, 8)).reshape(
        slots_here, 8 * potentials * rows_axis * rad_local, -1
    )
    product = jnp.einsum("jmh,jhk->jmk", folded, legendre, preferred_element_type=jnp.float32)
    product = product.reshape(slots_here, 2, 2, 2, potentials, rows_axis * rad_local, degrees)
    chosen = select_columns(product, own_pairs, degrees).astype(jnp.bfloat16)
    spectral = jnp.transpose(chosen, (2, 1, 0, 3, 4))
    degree = degree_table(own_pairs, degrees)[2]
    horizontal = ((degree * (degree + 1)).astype(jnp.float32) / (degrees * degrees))[
        None, :, None, :
    ]
    inverse = inv_radius[:, None]
    first_matrix = derivative_matrix(stencil_start, first_weights)
    second_matrix = derivative_matrix(stencil_start, second_weights)
    widened = spectral.astype(jnp.float32)
    current = curl_parts(widened[0], widened[1], first_matrix, second_matrix, horizontal, inverse)
    vorticity = curl_parts(widened[2], widened[3], first_matrix, second_matrix, horizontal, inverse)
    return (current, vorticity)


def order_table(pairs, degrees, points):
    q = np.arange(pairs)
    orders = np.stack([q, degrees - q], axis=0)
    phase = (orders[:, :, None] * np.arange(points // 2)[None, None, :]) % points
    angle = phase * (2.0 * np.pi / points)
    waves = np.stack([np.cos(angle), -np.sin(angle)], axis=1) / math.sqrt(points)
    waves = waves.reshape(2, 2, pairs // 2, 2, points // 2)
    waves = np.transpose(waves, (3, 0, 1, 2, 4)).reshape(2, 2 * pairs, points // 2)
    return waves.astype(np.float32).astype(ml_dtypes.bfloat16)


def kernel(
    dims,
    pairs_ref,
    start_ref,
    first_ref,
    second_ref,
    inverse_ref,
    pair_row_ref,
    grid_ref,
    table_hbm,
    legendre_hbm,
    current_ref,
    vorticity_ref,
    fields,
    table,
    legendre,
    halves,
    chosen,
    orders,
    wide,
    send,
    recv,
    mirrored,
    staged,
    grid_sem,
    table_sem,
    legendre_sem,
    own_sem,
    out_sem,
    send_a,
    recv_a,
    send_b,
    recv_b,
):
    n_ma, n_row, slots, lat, points, degrees, pairs, groups = dims
    devices = n_ma * n_row
    in_group = slots // groups
    half = points // 2
    lanes = lat // 128
    my_ma, my_row = lax.axis_index("ma"), lax.axis_index("row")
    me = my_ma * n_row + my_row

    def offset(i):
        t = i // n_ma
        step = ((t + 1) // 2) * (2 * (t % 2) - 1)
        return (i + 1) % n_ma, (n_row // 2 + step + n_row) % n_row

    def target(i):
        d_ma, d_row = offset(i)
        return (my_ma + d_ma) % n_ma, (my_row + d_row) % n_row

    def source(i):
        d_ma, d_row = offset(i)
        return (my_ma - d_ma + n_ma) % n_ma, (my_row - d_row + n_row) % n_row

    barrier = pltpu.get_barrier_semaphore()

    def greet(i, _):
        pl.semaphore_signal(barrier, inc=1, device_id=target(i), device_id_type=MESH)
        return 0

    lax.fori_loop(0, devices - 1, greet, 0)

    def load_table():
        return pltpu.make_async_copy(table_hbm, table, table_sem)

    def load_fields(f, r):
        return pltpu.make_async_copy(
            grid_ref.at[f, r], fields.at[f, r], grid_sem.at[f, r]
        )

    def load_legendre(j):
        return pltpu.make_async_copy(legendre_hbm.at[j], legendre.at[j], legendre_sem.at[j])

    load_table().start()
    for f in (0, 1):
        for r in (0, 1):
            load_fields(f, r).start()
    for f in (2, 3):
        for r in (0, 1):
            load_fields(f, r).start()
    for j in range(slots):
        load_legendre(j).start()

    def analyse(chunk):
        def one_radius(r, _):
            for f in (0, 1):
                load_fields(2 * chunk + f, r).wait()
                for rows in range(0, lat, 128):
                    for cols in range(0, half, 512):
                        west = fields[2 * chunk + f, r, rows : rows + 128, cols : cols + 512]
                        east = fields[
                            2 * chunk + f, r, rows : rows + 128, half + cols : half + cols + 512
                        ]
                        place = (slice(f * lat + rows, f * lat + rows + 128), slice(cols, cols + 512))
                        halves[(0,) + place] = west + east
                        halves[(1,) + place] = west - east
            count = pairs // 2
            for e in (0, 1):
                values = lax.dot_general(
                    table[e], halves[e], (((1,), (1,)), ((), ())), preferred_element_type=F32
                ).astype(BF16)
                for sc in range(4):
                    orders[e * count : (e + 1) * count, sc * 2 * lat : (sc + 1) * 2 * lat] = values[
                        sc * count : (sc + 1) * count
                    ]
            for sc in range(4):
                values = jnp.dot(
                    chosen[...],
                    orders[:, sc * 2 * lat : (sc + 1) * 2 * lat],
                    preferred_element_type=F32,
                )
                for f in (0, 1):
                    for t in range(lanes):
                        wide[t, pl.ds(r * 8 + f * 4 + sc, pairs, stride=16), :] = values[
                            :, f * lat + t * 128 : f * lat + (t + 1) * 128
                        ]
            return 0

        lax.fori_loop(0, 2, one_radius, 0)

    def pick(chunk, who, first, count):
        rows = pl.ds(pl.multiple_of((who * slots + first) * 16, 16), count * 16)
        for t in range(lanes):
            send[chunk, who, pl.ds(first, count), :, t * 128 : (t + 1) * 128] = (
                wide[t, rows, :].astype(BF16).reshape(count, 16, 128)
            )

    def copy_a(i, place, slot):
        return pltpu.make_async_remote_copy(
            src_ref=send.at[0, place[0] * n_row + place[1]],
            dst_ref=recv.at[0, slot],
            send_sem=send_a.at[i],
            recv_sem=recv_a.at[i],
            device_id=place,
            device_id_type=MESH,
        )

    def copy_b(i, g, place, slot):
        return pltpu.make_async_remote_copy(
            src_ref=send.at[1, place[0] * n_row + place[1], pl.ds(g * in_group, in_group)],
            dst_ref=recv.at[1, slot, pl.ds(g * in_group, in_group)],
            send_sem=send_b.at[g, i],
            recv_sem=recv_b.at[g, i],
            device_id=place,
            device_id_type=MESH,
        )

    def copy_own(chunk):
        return pltpu.make_async_copy(send.at[chunk, me], recv.at[chunk, me], own_sem.at[chunk])

    kind = lax.broadcasted_iota(jnp.int32, (pairs, 1), 0)
    kind = jnp.where(kind < pairs // 2, 2 * kind, 2 * kind - pairs + 1)
    by_order = jnp.where(kind == pair_row_ref[...], 1.0, 0.0).astype(F32)
    chosen[...] = by_order.T.astype(BF16)
    load_table().wait()
    analyse(0)
    pl.semaphore_wait(barrier, devices - 1)

    def send_first(i, _):
        place = target(i)
        pick(0, place[0] * n_row + place[1], 0, slots)
        copy_a(i, place, me).start()
        return 0

    lax.fori_loop(0, devices - 1, send_first, 0)
    pick(0, me, 0, slots)
    copy_own(0).start()

    analyse(1)

    def send_group(g, _):
        def one(i, _):
            place = target(i)
            pick(1, place[0] * n_row + place[1], g * in_group, in_group)
            copy_b(i, g, place, me).start()
            return 0

        lax.fori_loop(0, devices - 1, one, 0)
        return 0

    lax.fori_loop(0, groups, send_group, 0)
    pick(1, me, 0, slots)
    copy_own(1).start()

    radii = n_row * 2
    out_row = lax.broadcasted_iota(jnp.int32, (8 * radii, 1), 0)
    in_row = lax.broadcasted_iota(jnp.int32, (1, 8 * radii), 1)
    of_part, of_radius = out_row // (2 * radii), out_row % radii
    at_radius = in_row // 8
    nothing = jnp.zeros((8 * radii, 8 * radii), F32)

    def add_radius(r, held):
        first, second, inverse = held
        inverse = jnp.where(of_radius == r, inverse_ref[r], inverse)
        for w in range(first_ref.shape[1]):
            here = (of_radius == r) & (at_radius == start_ref[r] + w)
            first = first + jnp.where(here, first_ref[r, w], 0.0)
            second = second + jnp.where(here, second_ref[r, w], 0.0)
        return first, second, inverse

    first_matrix, second_matrix, inverse = lax.fori_loop(
        0, radii, add_radius, (nothing, nothing, jnp.zeros((8 * radii, 1), F32))
    )
    diagonal = jnp.where(of_radius == at_radius, inverse, 0.0)
    matrix = jnp.where(
        of_part < 2,
        diagonal + jnp.where(of_part == 1, first_matrix, 0.0),
        jnp.where(
            of_part == 2, -(second_matrix + 2.0 * inverse * first_matrix), diagonal * inverse
        ),
    )
    joined = ((in_row // 4) % 2 == jnp.where(of_part < 2, 1, 0)) & (
        in_row % 2 == (out_row // radii) % 2
    )
    matrix = jnp.where(joined, matrix, 0.0)
    matrix_high = matrix.astype(BF16)
    matrix_low = (matrix - matrix_high.astype(F32)).astype(BF16)
    column = lax.broadcasted_iota(jnp.int32, (1, degrees), 1)
    depth = legendre.shape[1]

    def of_slot(j):
        q = pairs_ref[me * slots + j]
        upper = column >= degrees - q
        order = jnp.where(upper, degrees - q, q)
        degree = jnp.where(upper, column, q + column)
        sign = 1.0 - 2.0 * ((degree - order) % 2).astype(F32)
        horizontal = (degree * (degree + 1)).astype(F32) / (degrees * degrees)
        return upper.astype(jnp.int32), sign, horizontal

    def mirror(j, k):
        sign = of_slot(j)[1]
        block = 256
        turn = (
            lax.broadcasted_iota(jnp.int32, (block, block), 0)
            + lax.broadcasted_iota(jnp.int32, (block, block), 1)
            == block - 1
        )
        turn = jnp.where(turn, 1.0, 0.0).astype(BF16)
        for b in range(depth // block):
            low = depth - (b + 1) * block
            values = jnp.dot(
                turn, legendre[j, low : low + block, :], preferred_element_type=F32
            )
            mirrored[k, b * block : (b + 1) * block, :] = (values * sign).astype(BF16)

    def out_copy(chunk, j):
        out = (current_ref, vorticity_ref)[chunk]
        return pltpu.make_async_copy(staged.at[chunk, j], out.at[:, :, j], out_sem.at[chunk, j])

    def transform(chunk, j, k):
        upper, _, horizontal = of_slot(j)
        north = n_ma // 2
        rows = [
            recv[chunk, a * n_row : (a + 1) * n_row, j].reshape(n_row * 16, lat)
            for a in range(n_ma)
        ]
        total = jnp.dot(
            jnp.concatenate(rows[:north], axis=1), legendre[j], preferred_element_type=F32
        ) + jnp.dot(
            jnp.concatenate(rows[north:], axis=1), mirrored[k], preferred_element_type=F32
        )
        side = lax.broadcasted_iota(jnp.int32, (n_row * 16, 1), 0) // 2 % 2
        modes = jnp.where(side == upper, total, 0.0).astype(BF16)
        result = jnp.dot(matrix_high, modes, preferred_element_type=F32) + jnp.dot(
            matrix_low, modes, preferred_element_type=F32
        )
        for c in (0, 1):
            at = c * radii
            staged[chunk, j, 0, c] = (result[at : at + radii] * horizontal).astype(BF16)
            at += 2 * radii
            staged[chunk, j, 1, c] = result[at : at + radii].astype(BF16)
            at += 2 * radii
            staged[chunk, j, 2, c] = (
                result[at : at + radii] + horizontal * result[at + 2 * radii : at + 3 * radii]
            ).astype(BF16)
        out_copy(chunk, j).start()

    for j in range(slots):
        load_legendre(j).wait()

    def wait_a(i, _):
        place = source(i)
        copy_a(i, target(i), place[0] * n_row + place[1]).wait_recv()
        return 0

    lax.fori_loop(0, devices - 1, wait_a, 0)
    copy_own(0).wait()

    def first(j, _):
        mirror(j, 0)
        transform(0, j, 0)
        return 0

    lax.fori_loop(0, slots, first, 0)
    copy_own(1).wait()

    def second(g, _):
        for k in range(in_group):
            mirror(g * in_group + k, k)

        def wait_b(i, _):
            place = source(i)
            copy_b(i, g, target(i), place[0] * n_row + place[1]).wait_recv()
            return 0

        lax.fori_loop(0, devices - 1, wait_b, 0)
        for k in range(in_group):
            transform(1, g * in_group + k, k)
        return 0

    lax.fori_loop(0, groups, second, 0)

    def sent(i, _):
        copy_a(i, target(i), me).wait_send()
        for g in range(groups):
            copy_b(i, g, target(i), me).wait_send()
        return 0

    lax.fori_loop(0, devices - 1, sent, 0)
    for chunk in (0, 1):
        for j in range(slots):
            out_copy(chunk, j).wait()


def kernel_shards(
    grid_fields, pair_list, legendre, stencil_start, first_weights, second_weights, inv_radius
):
    _, _, lat, points = grid_fields.shape
    slots, depth, degrees = legendre.shape
    n_ma, n_row = lax.axis_size("ma"), lax.axis_size("row")
    devices = n_ma * n_row
    pairs = pair_list.shape[0]
    radii = 2 * n_row
    groups = slots // 2
    table = jnp.asarray(order_table(pairs, degrees, points))
    out = jax.ShapeDtypeStruct((3, 2, slots, radii, degrees), BF16)
    anywhere = pl.BlockSpec(memory_space=pl.ANY)
    dims = (n_ma, n_row, slots, lat, points, degrees, pairs, groups)
    macs = 2 * 8 * lat * points // 2 * pairs * 4 // 2 + 2 * slots * 128 * 2 * depth * degrees
    return pl.pallas_call(
        functools.partial(kernel, dims),
        out_shape=(out, out),
        in_specs=[pl.BlockSpec(memory_space=pltpu.SMEM)] * 5
        + [pl.BlockSpec(memory_space=pltpu.VMEM)]
        + [anywhere] * 3,
        out_specs=(anywhere, anywhere),
        scratch_shapes=[
            pltpu.VMEM((4, 2, lat, points), BF16),
            pltpu.VMEM(table.shape, BF16),
            pltpu.VMEM((slots, depth, degrees), BF16),
            pltpu.VMEM((2, 2 * lat, points // 2), BF16),
            pltpu.VMEM((pairs, pairs), BF16),
            pltpu.VMEM((pairs, 8 * lat), BF16),
            pltpu.VMEM((lat // 128, pairs * 16, 128), F32),
            pltpu.VMEM((2, devices, slots, 16, lat), BF16),
            pltpu.VMEM((2, devices, slots, 16, lat), BF16),
            pltpu.VMEM((2, depth, degrees), BF16),
            pltpu.VMEM((2, slots, 3, 2, radii, degrees), BF16),
            pltpu.SemaphoreType.DMA((4, 2)),
            pltpu.SemaphoreType.DMA,
            pltpu.SemaphoreType.DMA((slots,)),
            pltpu.SemaphoreType.DMA((2,)),
            pltpu.SemaphoreType.DMA((2, slots)),
            pltpu.SemaphoreType.DMA((devices,)),
            pltpu.SemaphoreType.DMA((devices,)),
            pltpu.SemaphoreType.DMA((groups, devices)),
            pltpu.SemaphoreType.DMA((groups, devices)),
        ],
        compiler_params=pltpu.CompilerParams(
            collective_id=0, has_side_effects=True, vmem_limit_bytes=60 * 2**20
        ),
        cost_estimate=pl.CostEstimate(
            flops=2 * macs, bytes_accessed=2 * (grid_fields.size + legendre.size), transcendentals=0
        ),
    )(
        pair_list,
        stencil_start,
        first_weights,
        second_weights,
        inv_radius,
        pair_list.reshape(1, pairs),
        grid_fields,
        table,
        legendre,
    )


def solution(mesh):
    in_specs = (P(None, "row", "ma", None), P(), P(("ma", "row"), None, None), P(), P(), P(), P())
    out_specs = (P(None, None, ("ma", "row"), None, None), P(None, None, ("ma", "row"), None, None))
    n_ma, n_row = mesh.shape["ma"], mesh.shape["row"]

    def shards(*args):
        potentials, rad_local, lat, points = args[0].shape
        slots, depth, degrees = args[2].shape
        fits = (
            potentials == 4
            and rad_local == 2
            and lat % 128 == 0
            and depth % 256 == 0
            and degrees % 128 == 0
            and points % 1024 == 0
            and slots % 2 == 0
            and n_ma % 2 == 0
            and n_row == 8
            and args[1].shape[0] % 32 == 0
        )
        return (kernel_shards if fits else plain_shards)(*args)

    return jax.shard_map(shards, mesh=mesh, in_specs=in_specs, out_specs=out_specs, check_vma=False)
```

```python
import functools
import math

import jax
import jax.numpy as jnp
import ml_dtypes
import numpy as np
from jax import lax
from jax.experimental import pallas as pl
from jax.experimental.pallas import tpu as pltpu
from jax.sharding import PartitionSpec as P

MESH = pl.DeviceIdType.MESH
F32 = jnp.float32
BF16 = jnp.bfloat16


def degree_table(pair_values, degrees):
    column = jnp.arange(degrees, dtype=jnp.int32)
    upper_side = column[None, :] >= (degrees - pair_values)[:, None]
    degree = jnp.where(upper_side, column[None, :], pair_values[:, None] + column[None, :])
    order_value = jnp.where(upper_side, degrees - pair_values[:, None], pair_values[:, None])
    parity = (degree - order_value) % 2
    return (upper_side.astype(jnp.int32), parity, degree)


def derivative_matrix(stencil_start, weights):
    radius_count, stencil_width = weights.shape
    target = stencil_start[:, None] + jnp.arange(stencil_width, dtype=jnp.int32)[None, :]
    matches = target[:, :, None] == jnp.arange(radius_count, dtype=jnp.int32)[None, None, :]
    return jnp.sum(jnp.where(matches, weights[:, :, None], 0.0), axis=1)


def fourier_table(pair_values, degrees, points):
    orders = jnp.stack([pair_values, degrees - pair_values], axis=1)
    stride = 128
    factor = 1.0 / math.sqrt(points)

    def waves(positions):
        phases = orders[:, :, None] * positions[None, None, :] % points
        angles = phases.astype(jnp.float32) * (2.0 * math.pi / points)
        return jnp.cos(angles), jnp.sin(angles)

    wide_cos, wide_sin = waves(jnp.arange(points // stride, dtype=jnp.int32) * stride)
    fine_cos, fine_sin = waves(jnp.arange(stride, dtype=jnp.int32))
    wide_cos, wide_sin = wide_cos[..., None] * factor, wide_sin[..., None] * factor
    fine_cos, fine_sin = fine_cos[:, :, None, :], fine_sin[:, :, None, :]
    cosine = wide_cos * fine_cos - wide_sin * fine_sin
    sine = wide_sin * fine_cos + wide_cos * fine_sin
    table = jnp.stack([cosine, -sine], axis=2).astype(jnp.bfloat16)
    return table.reshape(pair_values.shape[0], 4, points)


def radial(matrix, values):
    return jnp.einsum("rt,cjtk->cjrk", matrix, values, precision=lax.Precision.HIGHEST)


def curl_parts(poloidal, toroidal, first_matrix, second_matrix, horizontal, inverse):
    poloidal_first = radial(first_matrix, poloidal)
    poloidal_second = radial(second_matrix, poloidal)
    toroidal_first = radial(first_matrix, toroidal)
    radial_part = horizontal * inverse * toroidal
    spheroidal = toroidal_first + inverse * toroidal
    toroidal_part = (
        -(poloidal_second + 2.0 * inverse * poloidal_first)
        + horizontal * inverse * inverse * poloidal
    )
    return jnp.stack([radial_part, spheroidal, toroidal_part], axis=0).astype(jnp.bfloat16)


def select_columns(product, pair_values, degrees):
    upper_side, parity, _ = degree_table(pair_values, degrees)
    wide = (slice(None),) + (None,) * 3 + (slice(None),)
    by_side = jnp.where(upper_side[:, None][wide] == 1, product[:, :, 1], product[:, :, 0])
    return jnp.where(parity[wide] == 1, by_side[:, 1], by_side[:, 0])


def plain_shards(
    grid_fields, pair_list, legendre, stencil_start, first_weights, second_weights, inv_radius
):
    potentials, rad_local, lat_local, points = grid_fields.shape
    degrees = legendre.shape[2]
    slots_here = legendre.shape[0]
    band_count = lax.axis_size("ma")
    rows_axis = lax.axis_size("row")
    fourier = fourier_table(pair_list, degrees, points)
    coefficients = jnp.einsum(
        "jsx,prhx->jsprh", fourier, grid_fields, preferred_element_type=jnp.float32
    ).astype(jnp.bfloat16)
    southern = lax.axis_index("ma") >= band_count // 2
    coefficients = jnp.where(southern, jnp.flip(coefficients, axis=-1), coefficients)
    at_owners = lax.all_to_all(
        coefficients, ("ma", "row"), split_axis=0, concat_axis=0, tiled=True
    ).reshape(band_count, rows_axis, slots_here, 2, 2, potentials, rad_local, lat_local)
    first_slot = (lax.axis_index("ma") * rows_axis + lax.axis_index("row")) * slots_here
    own_pairs = lax.dynamic_slice_in_dim(pair_list, first_slot, slots_here, 0)
    widened = at_owners.astype(jnp.float32)
    north = widened[: band_count // 2]
    south = jnp.flip(widened[band_count // 2 :], axis=0)
    folded = jnp.stack([north + south, north - south], axis=0).astype(jnp.bfloat16)
    folded = jnp.transpose(folded, (3, 0, 4, 5, 6, 2, 7, 1, 8)).reshape(
        slots_here, 8 * potentials * rows_axis * rad_local, -1
    )
    product = jnp.einsum("jmh,jhk->jmk", folded, legendre, preferred_element_type=jnp.float32)
    product = product.reshape(slots_here, 2, 2, 2, potentials, rows_axis * rad_local, degrees)
    chosen = select_columns(product, own_pairs, degrees).astype(jnp.bfloat16)
    spectral = jnp.transpose(chosen, (2, 1, 0, 3, 4))
    degree = degree_table(own_pairs, degrees)[2]
    horizontal = ((degree * (degree + 1)).astype(jnp.float32) / (degrees * degrees))[
        None, :, None, :
    ]
    inverse = inv_radius[:, None]
    first_matrix = derivative_matrix(stencil_start, first_weights)
    second_matrix = derivative_matrix(stencil_start, second_weights)
    widened = spectral.astype(jnp.float32)
    current = curl_parts(widened[0], widened[1], first_matrix, second_matrix, horizontal, inverse)
    vorticity = curl_parts(widened[2], widened[3], first_matrix, second_matrix, horizontal, inverse)
    return (current, vorticity)


def order_table(pairs, degrees, points):
    q = np.arange(pairs)
    orders = np.stack([q, degrees - q], axis=0)
    phase = (orders[:, :, None] * np.arange(points // 2)[None, None, :]) % points
    angle = phase * (2.0 * np.pi / points)
    waves = np.stack([np.cos(angle), -np.sin(angle)], axis=1) / math.sqrt(points)
    waves = waves.reshape(2, 2, pairs // 2, 2, points // 2)
    waves = np.transpose(waves, (3, 0, 1, 2, 4)).reshape(2, 2 * pairs, points // 2)
    return waves.astype(np.float32).astype(ml_dtypes.bfloat16)


def kernel(
    dims,
    pairs_ref,
    start_ref,
    inverse_ref,
    pair_row_ref,
    first_hbm,
    second_hbm,
    grid_hbm,
    table_hbm,
    legendre_hbm,
    current_ref,
    vorticity_ref,
    first_ref,
    second_ref,
    table,
    legendre,
    shared,
    halves,
    chosen,
    orders,
    wide,
    send,
    recv,
    weight_sem,
    grid_sem,
    table_sem,
    legendre_sem,
    own_sem,
    send_a,
    recv_a,
    send_b,
    recv_b,
):
    n_ma, n_row, slots, lat, half, degrees, pairs, groups = dims
    devices = n_ma * n_row
    tiles = lat // 128
    my_ma, my_row = lax.axis_index("ma"), lax.axis_index("row")
    me = my_ma * n_row + my_row

    def partner(i):
        far = n_row // 2
        mask = i % far + far * (1 - i // (devices // 2)) + n_row * (i % (devices // 2) // far)
        mask = lax.rem(mask, devices)
        place = 0
        bit = 1
        while bit < devices:
            place = place + bit * lax.rem(lax.div(me, bit) + lax.div(mask, bit), 2)
            bit *= 2
        return place

    def partner_of(n):
        return partner(n + n // (devices // 2))

    def mesh_place(place):
        return lax.div(place, n_row), lax.rem(place, n_row)

    barrier = pltpu.get_barrier_semaphore()

    def greet(n, _):
        place = mesh_place(partner_of(n))
        pl.semaphore_signal(barrier, inc=1, device_id=place, device_id_type=MESH)
        return 0

    lax.fori_loop(0, devices - 1, greet, 0)

    def load_table():
        return pltpu.make_async_copy(table_hbm, table, table_sem)

    def load_fields(f, r, t, side):
        return pltpu.make_async_copy(
            grid_hbm.at[f, r, pl.ds(t * 128, 128), pl.ds(side * half, half)],
            shared.at[f * 2 + r, pl.ds(side * lat + t * 128, 128)],
            grid_sem.at[f, r, t, side],
        )

    def load_weights():
        return (
            pltpu.make_async_copy(first_hbm, first_ref, weight_sem.at[0]),
            pltpu.make_async_copy(second_hbm, second_ref, weight_sem.at[1]),
        )

    def load_legendre(j):
        return pltpu.make_async_copy(legendre_hbm.at[j], legendre.at[j], legendre_sem.at[j])

    def start_fields(chunk, t):
        for r in (0, 1):
            for f in (0, 1):
                for side in (0, 1):
                    load_fields(2 * chunk + f, r, t, side).start()

    load_table().start()
    for t in range(tiles):
        start_fields(0, t)

    def analyse(chunk, t):
        count = pairs // 2
        for r in (0, 1):
            for f in (0, 1):
                which = 4 * chunk + f * 2 + r
                for side in (0, 1):
                    load_fields(2 * chunk + f, r, t, side).wait()
                for cols in range(0, half, 512):
                    west = shared[which, pl.ds(t * 128, 128), cols : cols + 512]
                    east = shared[which, pl.ds(lat + t * 128, 128), cols : cols + 512]
                    place = (slice((r * 2 + f) * 128, (r * 2 + f + 1) * 128), slice(cols, cols + 512))
                    halves[(0,) + place] = west + east
                    halves[(1,) + place] = west - east
        for e in (0, 1):
            values = lax.dot_general(
                table[e], halves[e], (((1,), (1,)), ((), ())), preferred_element_type=F32
            ).astype(BF16)
            for sc in range(4):
                orders[e * count : (e + 1) * count, sc * 512 : (sc + 1) * 512] = values[
                    sc * count : (sc + 1) * count
                ]
        for sc in range(4):
            values = jnp.dot(
                chosen[...],
                orders[:, sc * 512 : (sc + 1) * 512],
                preferred_element_type=F32,
            )
            for rf in range(4):
                wide[pl.ds(rf * 4 + sc, pairs, stride=16), :] = values[
                    :, rf * 128 : (rf + 1) * 128
                ]

    def pick(chunk, t, who):
        rows = pl.ds(pl.multiple_of(who * (slots * 16), slots * 16), slots * 16)
        send[chunk, t, who] = wide[rows, :].astype(BF16).reshape(slots, 16, 128)

    def copy_a(t, place):
        return pltpu.make_async_remote_copy(
            src_ref=send.at[0, t, place],
            dst_ref=recv.at[0, t, me],
            send_sem=send_a.at[t],
            recv_sem=recv_a.at[t],
            device_id=mesh_place(place),
            device_id_type=MESH,
        )

    def copy_b(g, place):
        part = pl.ds(*groups[g])
        return pltpu.make_async_remote_copy(
            src_ref=send.at[1, :, place, part],
            dst_ref=recv.at[1, :, me, part],
            send_sem=send_b.at[g],
            recv_sem=recv_b.at[g],
            device_id=mesh_place(place),
            device_id_type=MESH,
        )

    def copy_own(chunk):
        return pltpu.make_async_copy(
            send.at[chunk, :, me], recv.at[chunk, :, me], own_sem.at[chunk]
        )

    def all_a(t, sem):
        some = pl.ds(0, devices - 1)
        pltpu.make_async_copy(send.at[0, t, some], recv.at[0, t, some], sem).wait()

    def all_b(g, sem):
        some, part = pl.ds(0, devices - 1), pl.ds(*groups[g])
        pltpu.make_async_copy(send.at[1, :, some, part], recv.at[1, :, some, part], sem).wait()

    kind = lax.broadcasted_iota(jnp.int32, (pairs, 1), 0)
    kind = jnp.where(kind < pairs // 2, 2 * kind, 2 * kind - pairs + 1)
    by_order = jnp.where(kind == pair_row_ref[...], 1.0, 0.0).astype(F32)
    chosen[...] = by_order.T.astype(BF16)
    load_table().wait()

    for t in range(tiles):
        analyse(0, t)
        if t == 0:
            for later in range(tiles):
                start_fields(1, later)
            pl.semaphore_wait(barrier, devices - 1)

        def send_tile(n, _):
            place = partner_of(n)
            pick(0, t, place)
            copy_a(t, place).start()
            return 0

        lax.fori_loop(0, devices - 1, send_tile, 0)
        pick(0, t, me)
    copy_own(0).start()
    for j in range(slots):
        load_legendre(j).start()
    for copy in load_weights():
        copy.start()

    def second_chunk(t, _):
        analyse(1, t)

        def one(who, _):
            pick(1, t, who)
            return 0

        lax.fori_loop(0, devices, one, 0)
        return 0

    lax.fori_loop(0, tiles, second_chunk, 0)
    for g in range(len(groups)):

        def send_group(n, _):
            copy_b(g, partner_of(n)).start()
            return 0

        lax.fori_loop(0, devices - 1, send_group, 0)
    copy_own(1).start()

    for copy in load_weights():
        copy.wait()
    radii = n_row * 2
    out_row = lax.broadcasted_iota(jnp.int32, (8 * radii, 1), 0)
    in_row = lax.broadcasted_iota(jnp.int32, (1, 8 * radii), 1)
    of_part, of_radius = out_row // (2 * radii), out_row % radii
    at_radius = in_row // 8

    def add_radius(r, held):
        start, inverse = held
        here = of_radius == r
        return jnp.where(here, start_ref[r], start), jnp.where(here, inverse_ref[r], inverse)

    start, inverse = lax.fori_loop(
        0,
        radii,
        add_radius,
        (jnp.zeros((8 * radii, 1), jnp.int32), jnp.zeros((8 * radii, 1), F32)),
    )
    lane = lax.broadcasted_iota(jnp.int32, (1, radii), 1)

    def per_row(values):
        return jnp.sum(jnp.where(lane == of_radius, values, 0.0), axis=1, keepdims=True)

    first_matrix = jnp.zeros((8 * radii, 8 * radii), F32)
    second_matrix = first_matrix
    for w in range(first_ref.shape[0]):
        here = at_radius == start + w
        first_matrix += jnp.where(here, per_row(first_ref[w : w + 1, :]), 0.0)
        second_matrix += jnp.where(here, per_row(second_ref[w : w + 1, :]), 0.0)
    diagonal = jnp.where(of_radius == at_radius, inverse, 0.0)
    matrix = jnp.where(
        of_part < 2,
        diagonal + jnp.where(of_part == 1, first_matrix, 0.0),
        jnp.where(
            of_part == 2, -(second_matrix + 2.0 * inverse * first_matrix), diagonal * inverse
        ),
    )
    joined = ((in_row // 4) % 2 == jnp.where(of_part < 2, 1, 0)) & (
        in_row % 2 == (out_row // radii) % 2
    )
    matrix = jnp.where(joined, matrix, 0.0)
    matrix_high = matrix.astype(BF16)
    matrix_low = (matrix - matrix_high.astype(F32)).astype(BF16)
    column = lax.broadcasted_iota(jnp.int32, (1, degrees), 1)
    depth = legendre.shape[1]

    def of_slot(j):
        q = pairs_ref[me * slots + j]
        upper = column >= degrees - q
        order = jnp.where(upper, degrees - q, q)
        degree = jnp.where(upper, column, q + column)
        sign = 1.0 - 2.0 * ((degree - order) % 2).astype(F32)
        horizontal = (degree * (degree + 1)).astype(F32) / (degrees * degrees)
        return upper.astype(jnp.int32), sign, horizontal

    def mirror(j, _):
        load_legendre(j).wait()
        sign = of_slot(j)[1]
        block = 256
        turn = (
            lax.broadcasted_iota(jnp.int32, (block, block), 0)
            + lax.broadcasted_iota(jnp.int32, (block, block), 1)
            == block - 1
        )
        turn = jnp.where(turn, 1.0, 0.0).astype(BF16)
        for b in range(depth // block):
            low = depth - (b + 1) * block
            values = jnp.dot(turn, legendre[j, low : low + block, :], preferred_element_type=F32)
            shared[j, b * block : (b + 1) * block, :] = (values * sign).astype(BF16)
        return 0

    lax.fori_loop(0, slots, mirror, 0)

    def transform(chunk, j):
        upper, _, horizontal = of_slot(j)
        rows = [
            recv[chunk, t, a * n_row : (a + 1) * n_row, j].reshape(n_row * 16, 128)
            for a in range(n_ma)
            for t in range(tiles)
        ]
        north = n_ma // 2 * tiles
        total = jnp.dot(
            jnp.concatenate(rows[:north], axis=1), legendre[j], preferred_element_type=F32
        ) + jnp.dot(jnp.concatenate(rows[north:], axis=1), shared[j], preferred_element_type=F32)
        side = lax.broadcasted_iota(jnp.int32, (n_row * 16, 1), 0) // 2 % 2
        modes = jnp.where(side == upper, total, 0.0).astype(BF16)
        result = jnp.dot(matrix_high, modes, preferred_element_type=F32) + jnp.dot(
            matrix_low, modes, preferred_element_type=F32
        )
        out = (current_ref, vorticity_ref)[chunk]
        for c in (0, 1):
            at = c * radii
            out[0, c, j] = (result[at : at + radii] * horizontal).astype(BF16)
            at += 2 * radii
            out[1, c, j] = result[at : at + radii].astype(BF16)
            at += 2 * radii
            out[2, c, j] = (
                result[at : at + radii] + horizontal * result[at + 2 * radii : at + 3 * radii]
            ).astype(BF16)

    for t in range(tiles):
        all_a(t, recv_a.at[t])
    copy_own(0).wait()

    def first(j, _):
        transform(0, j)
        return 0

    lax.fori_loop(0, slots, first, 0)
    copy_own(1).wait()
    for t in range(tiles):
        all_a(t, send_a.at[t])
    for g in range(len(groups)):
        if g > 0:
            all_b(g - 1, send_b.at[g - 1])
        all_b(g, recv_b.at[g])

        def second(k, _):
            transform(1, groups[g][0] + k)
            return 0

        lax.fori_loop(0, groups[g][1], second, 0)
    all_b(len(groups) - 1, send_b.at[len(groups) - 1])


def write_kernel(current, vorticity, current_hbm, vorticity_hbm, sem):
    copies = []
    for o, (values, out) in enumerate(((current, current_hbm), (vorticity, vorticity_hbm))):
        for part in range(3):
            for c in (0, 1):
                copies.append(
                    pltpu.make_async_copy(
                        values.at[part, c], out.at[part, c], sem.at[o, part, c]
                    )
                )
    for copy in copies:
        copy.start()
    for copy in copies:
        copy.wait()


def kernel_shards(
    grid_fields, pair_list, legendre, stencil_start, first_weights, second_weights, inv_radius
):
    _, _, lat, points = grid_fields.shape
    slots, depth, degrees = legendre.shape
    n_ma, n_row = lax.axis_size("ma"), lax.axis_size("row")
    devices = n_ma * n_row
    pairs = pair_list.shape[0]
    radii = 2 * n_row
    tiles = lat // 128
    half = points // 2
    groups = [(0, slots // 2), (slots // 2, slots // 2 - 2), (slots - 2, 1), (slots - 1, 1)]
    groups = [g for g in groups if g[1] > 0]
    table = jnp.asarray(order_table(pairs, degrees, points))
    out_dims = (3, 2, slots, radii, degrees)
    anywhere = pl.BlockSpec(memory_space=pl.ANY)
    dims = (n_ma, n_row, slots, lat, half, degrees, pairs, groups)
    macs = 8 * lat * half * pairs * 4 + 2 * slots * 128 * 2 * depth * degrees
    current, vorticity = pl.pallas_call(
        functools.partial(kernel, dims),
        out_shape=(pltpu.VMEM(out_dims, BF16), pltpu.VMEM(out_dims, BF16)),
        in_specs=[pl.BlockSpec(memory_space=pltpu.SMEM)] * 3
        + [pl.BlockSpec(memory_space=pltpu.VMEM)]
        + [anywhere] * 5,
        out_specs=(pl.BlockSpec(memory_space=pltpu.VMEM),) * 2,
        scratch_shapes=[
            pltpu.VMEM(first_weights.shape[::-1], F32),
            pltpu.VMEM(second_weights.shape[::-1], F32),
            pltpu.VMEM(table.shape, BF16),
            pltpu.VMEM((slots, depth, degrees), BF16),
            pltpu.VMEM((8, 2 * lat, half), BF16),
            pltpu.VMEM((2, 512, half), BF16),
            pltpu.VMEM((pairs, pairs), BF16),
            pltpu.VMEM((pairs, 2048), BF16),
            pltpu.VMEM((pairs * 16, 128), F32),
            pltpu.VMEM((2, tiles, devices, slots, 16, 128), BF16),
            pltpu.VMEM((2, tiles, devices, slots, 16, 128), BF16),
            pltpu.SemaphoreType.DMA((2,)),
            pltpu.SemaphoreType.DMA((4, 2, tiles, 2)),
            pltpu.SemaphoreType.DMA,
            pltpu.SemaphoreType.DMA((slots,)),
            pltpu.SemaphoreType.DMA((2,)),
            pltpu.SemaphoreType.DMA((tiles,)),
            pltpu.SemaphoreType.DMA((tiles,)),
            pltpu.SemaphoreType.DMA((len(groups),)),
            pltpu.SemaphoreType.DMA((len(groups),)),
        ],
        compiler_params=pltpu.CompilerParams(
            collective_id=0, has_side_effects=True, vmem_limit_bytes=54 * 2**20
        ),
        cost_estimate=pl.CostEstimate(
            flops=2 * macs, bytes_accessed=2 * (grid_fields.size + legendre.size), transcendentals=0
        ),
    )(
        pair_list,
        stencil_start,
        inv_radius,
        pair_list.reshape(1, pairs),
        first_weights.T,
        second_weights.T,
        grid_fields,
        table,
        legendre,
    )
    out = jax.ShapeDtypeStruct(out_dims, BF16)
    return pl.pallas_call(
        write_kernel,
        out_shape=(out, out),
        in_specs=[pl.BlockSpec(memory_space=pltpu.VMEM)] * 2,
        out_specs=(anywhere, anywhere),
        scratch_shapes=[pltpu.SemaphoreType.DMA((2, 3, 2))],
    )(
        pltpu.with_memory_space_constraint(current, pltpu.VMEM),
        pltpu.with_memory_space_constraint(vorticity, pltpu.VMEM),
    )


def solution(mesh):
    in_specs = (P(None, "row", "ma", None), P(), P(("ma", "row"), None, None), P(), P(), P(), P())
    out_specs = (P(None, None, ("ma", "row"), None, None), P(None, None, ("ma", "row"), None, None))
    n_ma, n_row = mesh.shape["ma"], mesh.shape["row"]

    def shards(*args):
        potentials, rad_local, lat, points = args[0].shape
        slots, depth, degrees = args[2].shape
        fits = (
            potentials == 4
            and rad_local == 2
            and lat % 128 == 0
            and depth % 256 == 0
            and degrees % 128 == 0
            and points % 1024 == 0
            and slots == 8
            and n_ma == 4
            and n_row == 8
            and args[1].shape[0] == 256
            and depth == 2 * lat
            and degrees == points // 2
        )
        return (kernel_shards if fits else plain_shards)(*args)

    return jax.shard_map(shards, mesh=mesh, in_specs=in_specs, out_specs=out_specs, check_vma=False)
```

```python
import functools
import math

import jax
import jax.numpy as jnp
import ml_dtypes
import numpy as np
from jax import lax
from jax.experimental import pallas as pl
from jax.experimental.pallas import tpu as pltpu
from jax.sharding import PartitionSpec as P

MESH = pl.DeviceIdType.MESH
F32 = jnp.float32
BF16 = jnp.bfloat16


def degree_table(pair_values, degrees):
    column = jnp.arange(degrees, dtype=jnp.int32)
    upper_side = column[None, :] >= (degrees - pair_values)[:, None]
    degree = jnp.where(upper_side, column[None, :], pair_values[:, None] + column[None, :])
    order_value = jnp.where(upper_side, degrees - pair_values[:, None], pair_values[:, None])
    parity = (degree - order_value) % 2
    return (upper_side.astype(jnp.int32), parity, degree)


def derivative_matrix(stencil_start, weights):
    radius_count, stencil_width = weights.shape
    target = stencil_start[:, None] + jnp.arange(stencil_width, dtype=jnp.int32)[None, :]
    matches = target[:, :, None] == jnp.arange(radius_count, dtype=jnp.int32)[None, None, :]
    return jnp.sum(jnp.where(matches, weights[:, :, None], 0.0), axis=1)


def fourier_table(pair_values, degrees, points):
    orders = jnp.stack([pair_values, degrees - pair_values], axis=1)
    stride = 128
    factor = 1.0 / math.sqrt(points)

    def waves(positions):
        phases = orders[:, :, None] * positions[None, None, :] % points
        angles = phases.astype(jnp.float32) * (2.0 * math.pi / points)
        return jnp.cos(angles), jnp.sin(angles)

    wide_cos, wide_sin = waves(jnp.arange(points // stride, dtype=jnp.int32) * stride)
    fine_cos, fine_sin = waves(jnp.arange(stride, dtype=jnp.int32))
    wide_cos, wide_sin = wide_cos[..., None] * factor, wide_sin[..., None] * factor
    fine_cos, fine_sin = fine_cos[:, :, None, :], fine_sin[:, :, None, :]
    cosine = wide_cos * fine_cos - wide_sin * fine_sin
    sine = wide_sin * fine_cos + wide_cos * fine_sin
    table = jnp.stack([cosine, -sine], axis=2).astype(jnp.bfloat16)
    return table.reshape(pair_values.shape[0], 4, points)


def radial(matrix, values):
    return jnp.einsum("rt,cjtk->cjrk", matrix, values, precision=lax.Precision.HIGHEST)


def curl_parts(poloidal, toroidal, first_matrix, second_matrix, horizontal, inverse):
    poloidal_first = radial(first_matrix, poloidal)
    poloidal_second = radial(second_matrix, poloidal)
    toroidal_first = radial(first_matrix, toroidal)
    radial_part = horizontal * inverse * toroidal
    spheroidal = toroidal_first + inverse * toroidal
    toroidal_part = (
        -(poloidal_second + 2.0 * inverse * poloidal_first)
        + horizontal * inverse * inverse * poloidal
    )
    return jnp.stack([radial_part, spheroidal, toroidal_part], axis=0).astype(jnp.bfloat16)


def select_columns(product, pair_values, degrees):
    upper_side, parity, _ = degree_table(pair_values, degrees)
    wide = (slice(None),) + (None,) * 3 + (slice(None),)
    by_side = jnp.where(upper_side[:, None][wide] == 1, product[:, :, 1], product[:, :, 0])
    return jnp.where(parity[wide] == 1, by_side[:, 1], by_side[:, 0])


def plain_shards(
    grid_fields, pair_list, legendre, stencil_start, first_weights, second_weights, inv_radius
):
    potentials, rad_local, lat_local, points = grid_fields.shape
    degrees = legendre.shape[2]
    slots_here = legendre.shape[0]
    band_count = lax.axis_size("ma")
    rows_axis = lax.axis_size("row")
    fourier = fourier_table(pair_list, degrees, points)
    coefficients = jnp.einsum(
        "jsx,prhx->jsprh", fourier, grid_fields, preferred_element_type=jnp.float32
    ).astype(jnp.bfloat16)
    southern = lax.axis_index("ma") >= band_count // 2
    coefficients = jnp.where(southern, jnp.flip(coefficients, axis=-1), coefficients)
    at_owners = lax.all_to_all(
        coefficients, ("ma", "row"), split_axis=0, concat_axis=0, tiled=True
    ).reshape(band_count, rows_axis, slots_here, 2, 2, potentials, rad_local, lat_local)
    first_slot = (lax.axis_index("ma") * rows_axis + lax.axis_index("row")) * slots_here
    own_pairs = lax.dynamic_slice_in_dim(pair_list, first_slot, slots_here, 0)
    widened = at_owners.astype(jnp.float32)
    north = widened[: band_count // 2]
    south = jnp.flip(widened[band_count // 2 :], axis=0)
    folded = jnp.stack([north + south, north - south], axis=0).astype(jnp.bfloat16)
    folded = jnp.transpose(folded, (3, 0, 4, 5, 6, 2, 7, 1, 8)).reshape(
        slots_here, 8 * potentials * rows_axis * rad_local, -1
    )
    product = jnp.einsum("jmh,jhk->jmk", folded, legendre, preferred_element_type=jnp.float32)
    product = product.reshape(slots_here, 2, 2, 2, potentials, rows_axis * rad_local, degrees)
    chosen = select_columns(product, own_pairs, degrees).astype(jnp.bfloat16)
    spectral = jnp.transpose(chosen, (2, 1, 0, 3, 4))
    degree = degree_table(own_pairs, degrees)[2]
    horizontal = ((degree * (degree + 1)).astype(jnp.float32) / (degrees * degrees))[
        None, :, None, :
    ]
    inverse = inv_radius[:, None]
    first_matrix = derivative_matrix(stencil_start, first_weights)
    second_matrix = derivative_matrix(stencil_start, second_weights)
    widened = spectral.astype(jnp.float32)
    current = curl_parts(widened[0], widened[1], first_matrix, second_matrix, horizontal, inverse)
    vorticity = curl_parts(widened[2], widened[3], first_matrix, second_matrix, horizontal, inverse)
    return (current, vorticity)


def order_table(pairs, degrees, points):
    q = np.arange(pairs)
    orders = np.stack([q, degrees - q], axis=0)
    phase = (orders[:, :, None] * np.arange(points // 2)[None, None, :]) % points
    angle = phase * (2.0 * np.pi / points)
    waves = np.stack([np.cos(angle), -np.sin(angle)], axis=1) / math.sqrt(points)
    waves = waves.reshape(2, 2, pairs // 2, 2, points // 2)
    waves = np.transpose(waves, (3, 0, 1, 2, 4)).reshape(2, 2 * pairs, points // 2)
    return waves.astype(np.float32).astype(ml_dtypes.bfloat16)


def kernel(
    dims,
    pairs_ref,
    start_ref,
    inverse_ref,
    pair_row_ref,
    first_hbm,
    second_hbm,
    grid_hbm,
    table_hbm,
    legendre_hbm,
    current_ref,
    vorticity_ref,
    first_ref,
    second_ref,
    table,
    legendre,
    shared,
    halves,
    chosen,
    orders,
    wide,
    out_a,
    out_b,
    in_a,
    in_b,
    weight_sem,
    grid_sem,
    table_sem,
    legendre_sem,
    own_sem,
    send_a,
    recv_a,
    send_b,
    recv_b,
):
    n_ma, n_row, slots, lat, half, degrees, pairs, groups = dims
    devices = n_ma * n_row
    tiles = lat // 128
    my_ma, my_row = lax.axis_index("ma"), lax.axis_index("row")
    me = my_ma * n_row + my_row

    def partner(i):
        far = n_row // 2
        mask = i % far + far * (1 - i // (devices // 2)) + n_row * (i % (devices // 2) // far)
        mask = lax.rem(mask, devices)
        place = 0
        bit = 1
        while bit < devices:
            place = place + bit * lax.rem(lax.div(me, bit) + lax.div(mask, bit), 2)
            bit *= 2
        return place

    def partner_of(n):
        return partner(n + n // (devices // 2))

    def mesh_place(place):
        return lax.div(place, n_row), lax.rem(place, n_row)

    barrier = pltpu.get_barrier_semaphore()

    def greet():
        steps = {}
        for name, size, mine in (("ma", n_ma, my_ma), ("row", n_row, my_row)):
            steps[name] = [
                (1 << b) * (1 - 2 * lax.rem(lax.div(mine, 1 << b), 2))
                for b in range(size.bit_length() - 1)
            ]
        for mask in range(devices - 1, 0, -1):
            ma, row = my_ma, my_row
            for b, step in enumerate(steps["row"]):
                row = row + step if mask >> b & 1 else row
            for b, step in enumerate(steps["ma"]):
                ma = ma + step if (mask // n_row) >> b & 1 else ma
            pl.semaphore_signal(barrier, inc=1, device_id=(ma, row), device_id_type=MESH)

    def load_table(e):
        return pltpu.make_async_copy(table_hbm.at[e], table.at[e], table_sem.at[e])

    def load_fields(f, r, t, side):
        return pltpu.make_async_copy(
            grid_hbm.at[f, r, pl.ds(t * 128, 128), pl.ds(side * half, half)],
            shared.at[f * 2 + r, pl.ds(side * lat + t * 128, 128)],
            grid_sem.at[f, r, t, side],
        )

    def load_weights():
        return (
            pltpu.make_async_copy(first_hbm, first_ref, weight_sem.at[0]),
            pltpu.make_async_copy(second_hbm, second_ref, weight_sem.at[1]),
        )

    def load_legendre(j):
        return pltpu.make_async_copy(legendre_hbm.at[j], legendre.at[j], legendre_sem.at[j])

    def start_fields(chunk, t):
        for r in (0, 1):
            for f in (0, 1):
                for side in (0, 1):
                    load_fields(2 * chunk + f, r, t, side).start()

    start_fields(0, 0)
    for e in (0, 1):
        load_table(e).start()
    greet()

    def analyse(chunk, t):
        count = pairs // 2
        for r in (0, 1):
            for f in (0, 1):
                which = 4 * chunk + f * 2 + r
                for side in (0, 1):
                    load_fields(2 * chunk + f, r, t, side).wait()
                for cols in range(0, half, 512):
                    west = shared[which, pl.ds(t * 128, 128), cols : cols + 512]
                    east = shared[which, pl.ds(lat + t * 128, 128), cols : cols + 512]
                    place = (slice((r * 2 + f) * 128, (r * 2 + f + 1) * 128), slice(cols, cols + 512))
                    halves[(0,) + place] = west + east
                    halves[(1,) + place] = west - east
        for e in (0, 1):
            if chunk == 0 and isinstance(t, int) and t == 0:
                load_table(e).wait()
            values = lax.dot_general(
                table[e], halves[e], (((1,), (1,)), ((), ())), preferred_element_type=F32
            ).astype(BF16)
            for sc in range(4):
                orders[e * count : (e + 1) * count, sc * 512 : (sc + 1) * 512] = values[
                    sc * count : (sc + 1) * count
                ]
        for sc in range(4):
            values = jnp.dot(
                chosen[...],
                orders[:, sc * 512 : (sc + 1) * 512],
                preferred_element_type=F32,
            )
            for rf in range(4):
                wide[pl.ds(rf * 4 + sc, pairs, stride=16), :] = values[
                    :, rf * 128 : (rf + 1) * 128
                ]

    def pick(chunk, t, who):
        rows = pl.ds(pl.multiple_of(who * (slots * 16), slots * 16), slots * 16)
        values = wide[rows, :].astype(BF16).reshape(slots, 16, 128)
        if chunk == 0:
            out_a[t, who] = values
        else:
            out_b[who, :, t] = values

    def copy_a(t, place):
        return pltpu.make_async_remote_copy(
            src_ref=out_a.at[t, place],
            dst_ref=in_a.at[t, me],
            send_sem=send_a.at[t],
            recv_sem=recv_a.at[t],
            device_id=mesh_place(place),
            device_id_type=MESH,
        )

    def copy_b(g, place):
        part = pl.ds(*groups[g])
        return pltpu.make_async_remote_copy(
            src_ref=out_b.at[place, part],
            dst_ref=in_b.at[me, part],
            send_sem=send_b.at[g],
            recv_sem=recv_b.at[g],
            device_id=mesh_place(place),
            device_id_type=MESH,
        )

    def copy_own(chunk):
        if chunk == 0:
            return pltpu.make_async_copy(out_a.at[:, me], in_a.at[:, me], own_sem.at[chunk])
        return pltpu.make_async_copy(out_b.at[me], in_b.at[me], own_sem.at[chunk])

    def all_a(t, sem):
        some = pl.ds(0, devices - 1)
        pltpu.make_async_copy(out_a.at[t, some], in_a.at[t, some], sem).wait()

    def all_b(g, sem):
        some, part = pl.ds(0, devices - 1), pl.ds(*groups[g])
        pltpu.make_async_copy(out_b.at[some, part], in_b.at[some, part], sem).wait()

    kind = lax.broadcasted_iota(jnp.int32, (pairs, 1), 0)
    kind = jnp.where(kind < pairs // 2, 2 * kind, 2 * kind - pairs + 1)
    by_order = jnp.where(kind == pair_row_ref[...], 1.0, 0.0).astype(F32)
    chosen[...] = by_order.T.astype(BF16)

    for t in range(tiles):
        analyse(0, t)
        if t == 0:
            for later in range(1, tiles):
                start_fields(0, later)
            for later in range(tiles):
                start_fields(1, later)
            pl.semaphore_wait(barrier, devices - 1)

        def send_tile(n, _):
            place = partner_of(n)
            pick(0, t, place)
            copy_a(t, place).start()
            return 0

        lax.fori_loop(0, devices - 1, send_tile, 0)
        pick(0, t, me)
    copy_own(0).start()
    for j in range(slots):
        load_legendre(j).start()
    for copy in load_weights():
        copy.start()

    def second_chunk(t, _):
        analyse(1, t)

        def one(who, _):
            pick(1, t, who)
            return 0

        lax.fori_loop(0, devices, one, 0)
        return 0

    lax.fori_loop(0, tiles, second_chunk, 0)
    for g in range(len(groups)):

        def send_group(n, _):
            copy_b(g, partner_of(n)).start()
            return 0

        lax.fori_loop(0, devices - 1, send_group, 0)
    copy_own(1).start()

    for copy in load_weights():
        copy.wait()
    radii = n_row * 2
    out_row = lax.broadcasted_iota(jnp.int32, (8 * radii, 1), 0)
    in_row = lax.broadcasted_iota(jnp.int32, (1, 8 * radii), 1)
    of_part, of_radius = out_row // (2 * radii), out_row % radii
    at_radius = in_row // 8

    def add_radius(r, held):
        start, inverse = held
        here = of_radius == r
        return jnp.where(here, start_ref[r], start), jnp.where(here, inverse_ref[r], inverse)

    start, inverse = lax.fori_loop(
        0,
        radii,
        add_radius,
        (jnp.zeros((8 * radii, 1), jnp.int32), jnp.zeros((8 * radii, 1), F32)),
    )
    lane = lax.broadcasted_iota(jnp.int32, (1, radii), 1)

    def per_row(values):
        return jnp.sum(jnp.where(lane == of_radius, values, 0.0), axis=1, keepdims=True)

    first_matrix = jnp.zeros((8 * radii, 8 * radii), F32)
    second_matrix = first_matrix
    for w in range(first_ref.shape[0]):
        here = at_radius == start + w
        first_matrix += jnp.where(here, per_row(first_ref[w : w + 1, :]), 0.0)
        second_matrix += jnp.where(here, per_row(second_ref[w : w + 1, :]), 0.0)
    diagonal = jnp.where(of_radius == at_radius, inverse, 0.0)
    matrix = jnp.where(
        of_part < 2,
        diagonal + jnp.where(of_part == 1, first_matrix, 0.0),
        jnp.where(
            of_part == 2, -(second_matrix + 2.0 * inverse * first_matrix), diagonal * inverse
        ),
    )
    joined = ((in_row // 4) % 2 == jnp.where(of_part < 2, 1, 0)) & (
        in_row % 2 == (out_row // radii) % 2
    )
    matrix = jnp.where(joined, matrix, 0.0)
    matrix_high = matrix.astype(BF16)
    matrix_low = (matrix - matrix_high.astype(F32)).astype(BF16)
    column = lax.broadcasted_iota(jnp.int32, (1, degrees), 1)
    depth = legendre.shape[1]

    def of_slot(j):
        q = pairs_ref[me * slots + j]
        upper = column >= degrees - q
        order = jnp.where(upper, degrees - q, q)
        degree = jnp.where(upper, column, q + column)
        sign = 1.0 - 2.0 * ((degree - order) % 2).astype(F32)
        horizontal = (degree * (degree + 1)).astype(F32) / (degrees * degrees)
        return upper.astype(jnp.int32), sign, horizontal

    def mirror(j, _):
        load_legendre(j).wait()
        sign = of_slot(j)[1]
        block = 256
        turn = (
            lax.broadcasted_iota(jnp.int32, (block, block), 0)
            + lax.broadcasted_iota(jnp.int32, (block, block), 1)
            == block - 1
        )
        turn = jnp.where(turn, 1.0, 0.0).astype(BF16)
        for b in range(depth // block):
            low = depth - (b + 1) * block
            values = jnp.dot(turn, legendre[j, low : low + block, :], preferred_element_type=F32)
            shared[j, b * block : (b + 1) * block, :] = (values * sign).astype(BF16)
        return 0

    lax.fori_loop(0, slots, mirror, 0)

    def transform(chunk, j):
        upper, _, horizontal = of_slot(j)
        rows = [
            (
                in_a[t, a * n_row : (a + 1) * n_row, j]
                if chunk == 0
                else in_b[a * n_row : (a + 1) * n_row, j, t]
            ).reshape(n_row * 16, 128)
            for a in range(n_ma)
            for t in range(tiles)
        ]
        north = n_ma // 2 * tiles
        total = jnp.dot(
            jnp.concatenate(rows[:north], axis=1), legendre[j], preferred_element_type=F32
        ) + jnp.dot(jnp.concatenate(rows[north:], axis=1), shared[j], preferred_element_type=F32)
        side = lax.broadcasted_iota(jnp.int32, (n_row * 16, 1), 0) // 2 % 2
        modes = jnp.where(side == upper, total, 0.0).astype(BF16)
        result = jnp.dot(matrix_high, modes, preferred_element_type=F32) + jnp.dot(
            matrix_low, modes, preferred_element_type=F32
        )
        out = (current_ref, vorticity_ref)[chunk]
        for c in (0, 1):
            at = c * radii
            out[0, c, j] = (result[at : at + radii] * horizontal).astype(BF16)
            at += 2 * radii
            out[1, c, j] = result[at : at + radii].astype(BF16)
            at += 2 * radii
            out[2, c, j] = (
                result[at : at + radii] + horizontal * result[at + 2 * radii : at + 3 * radii]
            ).astype(BF16)

    for t in range(tiles):
        all_a(t, recv_a.at[t])
    copy_own(0).wait()

    def first(j, _):
        transform(0, j)
        return 0

    lax.fori_loop(0, slots, first, 0)
    copy_own(1).wait()
    for t in range(tiles):
        all_a(t, send_a.at[t])
    for g in range(len(groups)):
        if g > 0:
            all_b(g - 1, send_b.at[g - 1])
        all_b(g, recv_b.at[g])

        def second(k, _):
            transform(1, groups[g][0] + k)
            return 0

        lax.fori_loop(0, groups[g][1], second, 0)
    all_b(len(groups) - 1, send_b.at[len(groups) - 1])


def write_kernel(current, vorticity, current_hbm, vorticity_hbm, sem):
    copies = []
    for o, (values, out) in enumerate(((current, current_hbm), (vorticity, vorticity_hbm))):
        for part in range(3):
            for c in (0, 1):
                copies.append(
                    pltpu.make_async_copy(
                        values.at[part, c], out.at[part, c], sem.at[o, part, c]
                    )
                )
    for copy in copies:
        copy.start()
    for copy in copies:
        copy.wait()


def kernel_shards(
    grid_fields, pair_list, legendre, stencil_start, first_weights, second_weights, inv_radius
):
    _, _, lat, points = grid_fields.shape
    slots, depth, degrees = legendre.shape
    n_ma, n_row = lax.axis_size("ma"), lax.axis_size("row")
    devices = n_ma * n_row
    pairs = pair_list.shape[0]
    radii = 2 * n_row
    tiles = lat // 128
    half = points // 2
    groups = [(0, slots // 2), (slots // 2, slots // 2 - 2), (slots - 2, 1), (slots - 1, 1)]
    groups = [g for g in groups if g[1] > 0]
    table = jnp.asarray(order_table(pairs, degrees, points))
    out_dims = (3, 2, slots, radii, degrees)
    anywhere = pl.BlockSpec(memory_space=pl.ANY)
    dims = (n_ma, n_row, slots, lat, half, degrees, pairs, groups)
    macs = 8 * lat * half * pairs * 4 + 2 * slots * 128 * 2 * depth * degrees
    current, vorticity = pl.pallas_call(
        functools.partial(kernel, dims),
        out_shape=(pltpu.VMEM(out_dims, BF16), pltpu.VMEM(out_dims, BF16)),
        in_specs=[pl.BlockSpec(memory_space=pltpu.SMEM)] * 3
        + [pl.BlockSpec(memory_space=pltpu.VMEM)]
        + [anywhere] * 5,
        out_specs=(pl.BlockSpec(memory_space=pltpu.VMEM),) * 2,
        scratch_shapes=[
            pltpu.VMEM(first_weights.shape[::-1], F32),
            pltpu.VMEM(second_weights.shape[::-1], F32),
            pltpu.VMEM(table.shape, BF16),
            pltpu.VMEM((slots, depth, degrees), BF16),
            pltpu.VMEM((8, 2 * lat, half), BF16),
            pltpu.VMEM((2, 512, half), BF16),
            pltpu.VMEM((pairs, pairs), BF16),
            pltpu.VMEM((pairs, 2048), BF16),
            pltpu.VMEM((pairs * 16, 128), F32),
            pltpu.VMEM((tiles, devices, slots, 16, 128), BF16),
            pltpu.VMEM((devices, slots, tiles, 16, 128), BF16),
            pltpu.VMEM((tiles, devices, slots, 16, 128), BF16),
            pltpu.VMEM((devices, slots, tiles, 16, 128), BF16),
            pltpu.SemaphoreType.DMA((2,)),
            pltpu.SemaphoreType.DMA((4, 2, tiles, 2)),
            pltpu.SemaphoreType.DMA((2,)),
            pltpu.SemaphoreType.DMA((slots,)),
            pltpu.SemaphoreType.DMA((2,)),
            pltpu.SemaphoreType.DMA((tiles,)),
            pltpu.SemaphoreType.DMA((tiles,)),
            pltpu.SemaphoreType.DMA((len(groups),)),
            pltpu.SemaphoreType.DMA((len(groups),)),
        ],
        compiler_params=pltpu.CompilerParams(
            collective_id=0, has_side_effects=True, vmem_limit_bytes=54 * 2**20
        ),
        cost_estimate=pl.CostEstimate(
            flops=2 * macs, bytes_accessed=2 * (grid_fields.size + legendre.size), transcendentals=0
        ),
    )(
        pair_list,
        stencil_start,
        inv_radius,
        pair_list.reshape(1, pairs),
        first_weights.T,
        second_weights.T,
        grid_fields,
        table,
        legendre,
    )
    out = jax.ShapeDtypeStruct(out_dims, BF16)
    return pl.pallas_call(
        write_kernel,
        out_shape=(out, out),
        in_specs=[pl.BlockSpec(memory_space=pltpu.VMEM)] * 2,
        out_specs=(anywhere, anywhere),
        scratch_shapes=[pltpu.SemaphoreType.DMA((2, 3, 2))],
    )(
        pltpu.with_memory_space_constraint(current, pltpu.VMEM),
        pltpu.with_memory_space_constraint(vorticity, pltpu.VMEM),
    )


def solution(mesh):
    in_specs = (P(None, "row", "ma", None), P(), P(("ma", "row"), None, None), P(), P(), P(), P())
    out_specs = (P(None, None, ("ma", "row"), None, None), P(None, None, ("ma", "row"), None, None))
    n_ma, n_row = mesh.shape["ma"], mesh.shape["row"]

    def shards(*args):
        potentials, rad_local, lat, points = args[0].shape
        slots, depth, degrees = args[2].shape
        fits = (
            potentials == 4
            and rad_local == 2
            and lat % 128 == 0
            and depth % 256 == 0
            and degrees % 128 == 0
            and points % 1024 == 0
            and slots == 8
            and n_ma == 4
            and n_row == 8
            and args[1].shape[0] == 256
            and depth == 2 * lat
            and degrees == points // 2
        )
        return (kernel_shards if fits else plain_shards)(*args)

    return jax.shard_map(shards, mesh=mesh, in_specs=in_specs, out_specs=out_specs, check_vma=False)
```

```python
import functools
import math

import jax
import jax.numpy as jnp
import ml_dtypes
import numpy as np
from jax import lax
from jax.experimental import pallas as pl
from jax.experimental.pallas import tpu as pltpu
from jax.sharding import PartitionSpec as P

MESH = pl.DeviceIdType.MESH
F32 = jnp.float32
BF16 = jnp.bfloat16


def degree_table(pair_values, degrees):
    column = jnp.arange(degrees, dtype=jnp.int32)
    upper_side = column[None, :] >= (degrees - pair_values)[:, None]
    degree = jnp.where(upper_side, column[None, :], pair_values[:, None] + column[None, :])
    order_value = jnp.where(upper_side, degrees - pair_values[:, None], pair_values[:, None])
    parity = (degree - order_value) % 2
    return (upper_side.astype(jnp.int32), parity, degree)


def derivative_matrix(stencil_start, weights):
    radius_count, stencil_width = weights.shape
    target = stencil_start[:, None] + jnp.arange(stencil_width, dtype=jnp.int32)[None, :]
    matches = target[:, :, None] == jnp.arange(radius_count, dtype=jnp.int32)[None, None, :]
    return jnp.sum(jnp.where(matches, weights[:, :, None], 0.0), axis=1)


def fourier_table(pair_values, degrees, points):
    orders = jnp.stack([pair_values, degrees - pair_values], axis=1)
    stride = 128
    factor = 1.0 / math.sqrt(points)

    def waves(positions):
        phases = orders[:, :, None] * positions[None, None, :] % points
        angles = phases.astype(jnp.float32) * (2.0 * math.pi / points)
        return jnp.cos(angles), jnp.sin(angles)

    wide_cos, wide_sin = waves(jnp.arange(points // stride, dtype=jnp.int32) * stride)
    fine_cos, fine_sin = waves(jnp.arange(stride, dtype=jnp.int32))
    wide_cos, wide_sin = wide_cos[..., None] * factor, wide_sin[..., None] * factor
    fine_cos, fine_sin = fine_cos[:, :, None, :], fine_sin[:, :, None, :]
    cosine = wide_cos * fine_cos - wide_sin * fine_sin
    sine = wide_sin * fine_cos + wide_cos * fine_sin
    table = jnp.stack([cosine, -sine], axis=2).astype(jnp.bfloat16)
    return table.reshape(pair_values.shape[0], 4, points)


def radial(matrix, values):
    return jnp.einsum("rt,cjtk->cjrk", matrix, values, precision=lax.Precision.HIGHEST)


def curl_parts(poloidal, toroidal, first_matrix, second_matrix, horizontal, inverse):
    poloidal_first = radial(first_matrix, poloidal)
    poloidal_second = radial(second_matrix, poloidal)
    toroidal_first = radial(first_matrix, toroidal)
    radial_part = horizontal * inverse * toroidal
    spheroidal = toroidal_first + inverse * toroidal
    toroidal_part = (
        -(poloidal_second + 2.0 * inverse * poloidal_first)
        + horizontal * inverse * inverse * poloidal
    )
    return jnp.stack([radial_part, spheroidal, toroidal_part], axis=0).astype(jnp.bfloat16)


def select_columns(product, pair_values, degrees):
    upper_side, parity, _ = degree_table(pair_values, degrees)
    wide = (slice(None),) + (None,) * 3 + (slice(None),)
    by_side = jnp.where(upper_side[:, None][wide] == 1, product[:, :, 1], product[:, :, 0])
    return jnp.where(parity[wide] == 1, by_side[:, 1], by_side[:, 0])


def plain_shards(
    grid_fields, pair_list, legendre, stencil_start, first_weights, second_weights, inv_radius
):
    potentials, rad_local, lat_local, points = grid_fields.shape
    degrees = legendre.shape[2]
    slots_here = legendre.shape[0]
    band_count = lax.axis_size("ma")
    rows_axis = lax.axis_size("row")
    fourier = fourier_table(pair_list, degrees, points)
    coefficients = jnp.einsum(
        "jsx,prhx->jsprh", fourier, grid_fields, preferred_element_type=jnp.float32
    ).astype(jnp.bfloat16)
    southern = lax.axis_index("ma") >= band_count // 2
    coefficients = jnp.where(southern, jnp.flip(coefficients, axis=-1), coefficients)
    at_owners = lax.all_to_all(
        coefficients, ("ma", "row"), split_axis=0, concat_axis=0, tiled=True
    ).reshape(band_count, rows_axis, slots_here, 2, 2, potentials, rad_local, lat_local)
    first_slot = (lax.axis_index("ma") * rows_axis + lax.axis_index("row")) * slots_here
    own_pairs = lax.dynamic_slice_in_dim(pair_list, first_slot, slots_here, 0)
    widened = at_owners.astype(jnp.float32)
    north = widened[: band_count // 2]
    south = jnp.flip(widened[band_count // 2 :], axis=0)
    folded = jnp.stack([north + south, north - south], axis=0).astype(jnp.bfloat16)
    folded = jnp.transpose(folded, (3, 0, 4, 5, 6, 2, 7, 1, 8)).reshape(
        slots_here, 8 * potentials * rows_axis * rad_local, -1
    )
    product = jnp.einsum("jmh,jhk->jmk", folded, legendre, preferred_element_type=jnp.float32)
    product = product.reshape(slots_here, 2, 2, 2, potentials, rows_axis * rad_local, degrees)
    chosen = select_columns(product, own_pairs, degrees).astype(jnp.bfloat16)
    spectral = jnp.transpose(chosen, (2, 1, 0, 3, 4))
    degree = degree_table(own_pairs, degrees)[2]
    horizontal = ((degree * (degree + 1)).astype(jnp.float32) / (degrees * degrees))[
        None, :, None, :
    ]
    inverse = inv_radius[:, None]
    first_matrix = derivative_matrix(stencil_start, first_weights)
    second_matrix = derivative_matrix(stencil_start, second_weights)
    widened = spectral.astype(jnp.float32)
    current = curl_parts(widened[0], widened[1], first_matrix, second_matrix, horizontal, inverse)
    vorticity = curl_parts(widened[2], widened[3], first_matrix, second_matrix, horizontal, inverse)
    return (current, vorticity)


def order_table(pairs, degrees, points):
    q = np.arange(pairs)
    orders = np.stack([q, degrees - q], axis=0)
    phase = (orders[:, :, None] * np.arange(points // 2)[None, None, :]) % points
    angle = phase * (2.0 * np.pi / points)
    waves = np.stack([np.cos(angle), -np.sin(angle)], axis=1) / math.sqrt(points)
    waves = waves.reshape(2, 2, pairs // 2, 2, points // 2)
    waves = np.transpose(waves, (3, 0, 1, 2, 4)).reshape(2, 2 * pairs, points // 2)
    waves = np.ascontiguousarray(np.swapaxes(waves, 1, 2))
    return waves.astype(np.float32).astype(ml_dtypes.bfloat16)


def curl(rows, tables, upper, horizontal, matrices):
    half = len(rows) // 2
    total = jnp.dot(
        jnp.concatenate(rows[:half], axis=1), tables[0], preferred_element_type=F32
    ) + jnp.dot(jnp.concatenate(rows[half:], axis=1), tables[1], preferred_element_type=F32)
    count = total.shape[0]
    side = lax.broadcasted_iota(jnp.int32, (count, 1), 0) // 2 % 2
    modes = jnp.where(side == upper, total, 0.0).astype(BF16)
    result = jnp.dot(matrices[0], modes, preferred_element_type=F32) + jnp.dot(
        matrices[1], modes, preferred_element_type=F32
    )
    radii = count // 8
    parts = {}
    for c in (0, 1):
        block = [result[(2 * p + c) * radii : (2 * p + c + 1) * radii] for p in range(4)]
        parts[0, c] = (block[0] * horizontal).astype(BF16)
        parts[1, c] = block[1].astype(BF16)
        parts[2, c] = (block[2] + horizontal * block[3]).astype(BF16)
    return parts


def kernel(
    dims,
    pairs_ref,
    start_ref,
    inverse_ref,
    pair_row_ref,
    first_hbm,
    second_hbm,
    grid_hbm,
    table_hbm,
    legendre_hbm,
    current_ref,
    vorticity_ref,
    last_in,
    last_tables,
    last_rows,
    matrices,
    first_ref,
    second_ref,
    table,
    legendre,
    shared,
    halves,
    chosen,
    orders,
    wide,
    out_a,
    out_b,
    in_a,
    in_b,
    weight_sem,
    grid_sem,
    table_sem,
    legendre_sem,
    own_sem,
    last_sem,
    send_a,
    recv_a,
    send_b,
    recv_b,
):
    n_ma, n_row, slots, lat, half, degrees, pairs, groups = dims
    devices = n_ma * n_row
    tiles = lat // 128
    my_ma, my_row = lax.axis_index("ma"), lax.axis_index("row")
    me = my_ma * n_row + my_row

    def partner(i):
        far = n_row // 2
        mask = i % far + far * (1 - i // (devices // 2)) + n_row * (i % (devices // 2) // far)
        mask = lax.rem(mask, devices)
        place = 0
        bit = 1
        while bit < devices:
            place = place + bit * lax.rem(lax.div(me, bit) + lax.div(mask, bit), 2)
            bit *= 2
        return place

    def partner_of(n):
        return partner(n + n // (devices // 2))

    def mesh_place(place):
        return lax.div(place, n_row), lax.rem(place, n_row)

    barrier = pltpu.get_barrier_semaphore()

    def greet():
        steps = {}
        for name, size, mine in (("ma", n_ma, my_ma), ("row", n_row, my_row)):
            steps[name] = [
                (1 << b) * (1 - 2 * lax.rem(lax.div(mine, 1 << b), 2))
                for b in range(size.bit_length() - 1)
            ]
        for mask in range(devices - 1, 0, -1):
            ma, row = my_ma, my_row
            for b, step in enumerate(steps["row"]):
                row = row + step if mask >> b & 1 else row
            for b, step in enumerate(steps["ma"]):
                ma = ma + step if (mask // n_row) >> b & 1 else ma
            pl.semaphore_signal(barrier, inc=1, device_id=(ma, row), device_id_type=MESH)

    def load_table(e):
        return pltpu.make_async_copy(table_hbm.at[e], table.at[e], table_sem.at[e])

    def load_fields(f, r, t, side):
        return pltpu.make_async_copy(
            grid_hbm.at[f, r, pl.ds(t * 128, 128), pl.ds(side * half, half)],
            shared.at[f * 2 + r, pl.ds(side * lat + t * 128, 128)],
            grid_sem.at[f, r, t, side],
        )

    def load_weights():
        return (
            pltpu.make_async_copy(first_hbm, first_ref, weight_sem.at[0]),
            pltpu.make_async_copy(second_hbm, second_ref, weight_sem.at[1]),
        )

    def load_legendre(j):
        return pltpu.make_async_copy(legendre_hbm.at[j], legendre.at[j], legendre_sem.at[j])

    def start_fields(chunk, t):
        for r in (0, 1):
            for f in (0, 1):
                for side in (0, 1):
                    load_fields(2 * chunk + f, r, t, side).start()

    start_fields(0, 0)
    for e in (0, 1):
        load_table(e).start()
    greet()

    def analyse(chunk, t):
        count = pairs // 2
        for r in (0, 1):
            for f in (0, 1):
                which = 4 * chunk + f * 2 + r
                for side in (0, 1):
                    load_fields(2 * chunk + f, r, t, side).wait()
                for cols in range(0, half, 512):
                    west = shared[which, pl.ds(t * 128, 128), cols : cols + 512]
                    east = shared[which, pl.ds(lat + t * 128, 128), cols : cols + 512]
                    place = (slice((r * 2 + f) * 128, (r * 2 + f + 1) * 128), slice(cols, cols + 512))
                    halves[(0,) + place] = west + east
                    halves[(1,) + place] = west - east
        for e in (0, 1):
            if chunk == 0 and isinstance(t, int) and t == 0:
                load_table(e).wait()
            values = jnp.dot(halves[e], table[e], preferred_element_type=F32).astype(BF16)
            for sc in range(4):
                at = sc * pairs + e * count
                orders[:, at : at + count] = values[:, sc * count : (sc + 1) * count]
        for sc in range(4):
            values = lax.dot_general(
                chosen[...],
                orders[:, sc * pairs : (sc + 1) * pairs],
                (((1,), (1,)), ((), ())),
                preferred_element_type=F32,
            )
            for rf in range(4):
                wide[pl.ds(rf * 4 + sc, pairs, stride=16), :] = values[
                    :, rf * 128 : (rf + 1) * 128
                ]

    def pick(chunk, t, who):
        rows = pl.ds(pl.multiple_of(who * (slots * 16), slots * 16), slots * 16)
        values = wide[rows, :].astype(BF16).reshape(slots, 16, 128)
        if chunk == 0:
            out_a[t, who] = values
        else:
            out_b[who, :, t] = values

    def copy_a(t, place):
        return pltpu.make_async_remote_copy(
            src_ref=out_a.at[t, place],
            dst_ref=in_a.at[t, me],
            send_sem=send_a.at[t],
            recv_sem=recv_a.at[t],
            device_id=mesh_place(place),
            device_id_type=MESH,
        )

    last = slots - 1

    def ends_b(g, source, target):
        if g == len(groups) - 1:
            return out_b.at[source, last], last_in.at[target]
        part = pl.ds(*groups[g])
        return out_b.at[source, part], in_b.at[target, part]

    def copy_b(g, place):
        source, target = ends_b(g, place, me)
        return pltpu.make_async_remote_copy(
            src_ref=source,
            dst_ref=target,
            send_sem=send_b.at[g],
            recv_sem=recv_b.at[g],
            device_id=mesh_place(place),
            device_id_type=MESH,
        )

    def copy_own(chunk):
        if chunk == 0:
            pairs_of_refs = [(out_a.at[:, me], in_a.at[:, me])]
        else:
            pairs_of_refs = [
                (out_b.at[me, pl.ds(0, last)], in_b.at[me]),
                (out_b.at[me, last], last_in.at[me]),
            ]
        return [
            pltpu.make_async_copy(source, target, own_sem.at[chunk + n])
            for n, (source, target) in enumerate(pairs_of_refs)
        ]

    def all_a(t, sem):
        some = pl.ds(0, devices - 1)
        pltpu.make_async_copy(out_a.at[t, some], in_a.at[t, some], sem).wait()

    def all_b(g, sem):
        some = pl.ds(0, devices - 1)
        pltpu.make_async_copy(*ends_b(g, some, some), sem).wait()

    kind = lax.broadcasted_iota(jnp.int32, (pairs, 1), 0)
    kind = jnp.where(kind < pairs // 2, 2 * kind, 2 * kind - pairs + 1)
    by_order = jnp.where(kind == pair_row_ref[...], 1.0, 0.0).astype(F32)
    chosen[...] = by_order.T.astype(BF16)

    for t in range(tiles):
        analyse(0, t)
        if t == 0:
            for later in range(1, tiles):
                start_fields(0, later)
            for later in range(tiles):
                start_fields(1, later)
            pl.semaphore_wait(barrier, devices - 1)

        def send_tile(n, _):
            place = partner_of(n)
            pick(0, t, place)
            copy_a(t, place).start()
            return 0

        lax.fori_loop(0, devices - 1, send_tile, 0)
        pick(0, t, me)
    for copy in copy_own(0):
        copy.start()
    for j in range(slots):
        load_legendre(j).start()
    for copy in load_weights():
        copy.start()

    def second_chunk(t, _):
        analyse(1, t)

        def one(who, _):
            pick(1, t, who)
            return 0

        lax.fori_loop(0, devices, one, 0)
        return 0

    lax.fori_loop(0, tiles, second_chunk, 0)
    for g in range(len(groups)):

        def send_group(n, _):
            copy_b(g, partner_of(n)).start()
            return 0

        lax.fori_loop(0, devices - 1, send_group, 0)
    for copy in copy_own(1):
        copy.start()

    for copy in load_weights():
        copy.wait()
    radii = n_row * 2
    out_row = lax.broadcasted_iota(jnp.int32, (8 * radii, 1), 0)
    in_row = lax.broadcasted_iota(jnp.int32, (1, 8 * radii), 1)
    of_part, of_radius = out_row // (2 * radii), out_row % radii
    at_radius = in_row // 8

    def add_radius(r, held):
        start, inverse = held
        here = of_radius == r
        return jnp.where(here, start_ref[r], start), jnp.where(here, inverse_ref[r], inverse)

    start, inverse = lax.fori_loop(
        0,
        radii,
        add_radius,
        (jnp.zeros((8 * radii, 1), jnp.int32), jnp.zeros((8 * radii, 1), F32)),
    )
    lane = lax.broadcasted_iota(jnp.int32, (1, radii), 1)

    def per_row(values):
        return jnp.sum(jnp.where(lane == of_radius, values, 0.0), axis=1, keepdims=True)

    first_matrix = jnp.zeros((8 * radii, 8 * radii), F32)
    second_matrix = first_matrix
    for w in range(first_ref.shape[0]):
        here = at_radius == start + w
        first_matrix += jnp.where(here, per_row(first_ref[w : w + 1, :]), 0.0)
        second_matrix += jnp.where(here, per_row(second_ref[w : w + 1, :]), 0.0)
    diagonal = jnp.where(of_radius == at_radius, inverse, 0.0)
    matrix = jnp.where(
        of_part < 2,
        diagonal + jnp.where(of_part == 1, first_matrix, 0.0),
        jnp.where(
            of_part == 2, -(second_matrix + 2.0 * inverse * first_matrix), diagonal * inverse
        ),
    )
    joined = ((in_row // 4) % 2 == jnp.where(of_part < 2, 1, 0)) & (
        in_row % 2 == (out_row // radii) % 2
    )
    matrix = jnp.where(joined, matrix, 0.0)
    matrix_high = matrix.astype(BF16)
    matrices[0] = matrix_high
    matrices[1] = (matrix - matrix_high.astype(F32)).astype(BF16)
    column = lax.broadcasted_iota(jnp.int32, (1, degrees), 1)
    depth = legendre.shape[1]

    def of_slot(j):
        q = pairs_ref[me * slots + j]
        upper = column >= degrees - q
        order = jnp.where(upper, degrees - q, q)
        degree = jnp.where(upper, column, q + column)
        sign = 1.0 - 2.0 * ((degree - order) % 2).astype(F32)
        horizontal = (degree * (degree + 1)).astype(F32) / (degrees * degrees)
        return upper.astype(jnp.int32), sign, horizontal

    def mirror(j, _):
        load_legendre(j).wait()
        sign = of_slot(j)[1]
        block = 256
        turn = (
            lax.broadcasted_iota(jnp.int32, (block, block), 0)
            + lax.broadcasted_iota(jnp.int32, (block, block), 1)
            == block - 1
        )
        turn = jnp.where(turn, 1.0, 0.0).astype(BF16)
        for b in range(depth // block):
            low = depth - (b + 1) * block
            values = jnp.dot(turn, legendre[j, low : low + block, :], preferred_element_type=F32)
            shared[j, b * block : (b + 1) * block, :] = (values * sign).astype(BF16)
        return 0

    lax.fori_loop(0, slots, mirror, 0)
    last_copies = [
        pltpu.make_async_copy(part.at[last], last_tables.at[n], last_sem.at[n])
        for n, part in enumerate((legendre, shared))
    ]
    for copy in last_copies:
        copy.start()
    upper, _, horizontal = of_slot(last)
    last_rows[0] = upper.astype(F32)
    last_rows[1] = horizontal

    def transform(chunk, j):
        upper, _, horizontal = of_slot(j)
        rows = [
            (
                in_a[t, a * n_row : (a + 1) * n_row, j]
                if chunk == 0
                else in_b[a * n_row : (a + 1) * n_row, j, t]
            ).reshape(n_row * 16, 128)
            for a in range(n_ma)
            for t in range(tiles)
        ]
        parts = curl(rows, (legendre[j], shared[j]), upper, horizontal, matrices)
        for (part, c), values in parts.items():
            (current_ref, vorticity_ref)[chunk][part, c, j] = values

    for t in range(tiles):
        all_a(t, recv_a.at[t])
    for copy in copy_own(0):
        copy.wait()

    def first(j, _):
        transform(0, j)
        return 0

    lax.fori_loop(0, slots, first, 0)
    for copy in copy_own(1):
        copy.wait()
    for t in range(tiles):
        all_a(t, send_a.at[t])
    for g in range(len(groups)):
        if g > 0:
            all_b(g - 1, send_b.at[g - 1])
        all_b(g, recv_b.at[g])

        def second(k, _):
            transform(1, groups[g][0] + k)
            return 0

        if g < len(groups) - 1:
            lax.fori_loop(0, groups[g][1], second, 0)
        if g == 0:
            for copy in last_copies:
                copy.wait()
    all_b(len(groups) - 1, send_b.at[len(groups) - 1])


def write_kernel(
    current, vorticity, last_in, last_tables, last_rows, matrices, current_hbm, vorticity_hbm,
    staged, sem, last_sem,
):
    last = vorticity.shape[2] - 1
    copies = []
    for part in range(3):
        for c in (0, 1):
            copies.append(
                pltpu.make_async_copy(
                    vorticity.at[part, c, pl.ds(0, last)],
                    vorticity_hbm.at[part, c, pl.ds(0, last)],
                    sem.at[0, part, c],
                )
            )
            copies.append(
                pltpu.make_async_copy(
                    current.at[part, c], current_hbm.at[part, c], sem.at[1, part, c]
                )
            )
    for copy in copies:
        copy.start()
    bands, count = 4, last_in.shape[0] // 4
    rows = [
        last_in[a * count : (a + 1) * count, t].reshape(count * 16, 128)
        for a in range(bands)
        for t in range(last_in.shape[1])
    ]
    upper = last_rows[0].astype(jnp.int32)
    parts = curl(rows, (last_tables[0], last_tables[1]), upper, last_rows[1], matrices)
    for (part, c), values in parts.items():
        staged[part, c] = values
        copy = pltpu.make_async_copy(
            staged.at[part, c], vorticity_hbm.at[part, c, last], last_sem.at[part, c]
        )
        copy.start()
        copies.append(copy)
    for copy in copies:
        copy.wait()


def kernel_shards(
    grid_fields, pair_list, legendre, stencil_start, first_weights, second_weights, inv_radius
):
    _, _, lat, points = grid_fields.shape
    slots, depth, degrees = legendre.shape
    n_ma, n_row = lax.axis_size("ma"), lax.axis_size("row")
    devices = n_ma * n_row
    pairs = pair_list.shape[0]
    radii = 2 * n_row
    tiles = lat // 128
    half = points // 2
    groups = [(0, slots // 2), (slots // 2, slots // 2 - 1), (slots - 1, 1)]
    table = jnp.asarray(order_table(pairs, degrees, points))
    out_dims = (3, 2, slots, radii, degrees)
    anywhere = pl.BlockSpec(memory_space=pl.ANY)
    dims = (n_ma, n_row, slots, lat, half, degrees, pairs, groups)
    macs = 8 * lat * half * pairs * 4 + 2 * slots * 128 * 2 * depth * degrees
    held = (
        pltpu.VMEM(out_dims, BF16),
        pltpu.VMEM(out_dims, BF16),
        pltpu.VMEM((devices, tiles, 16, 128), BF16),
        pltpu.VMEM((2, depth, degrees), BF16),
        pltpu.VMEM((2, 1, degrees), F32),
        pltpu.VMEM((2, 8 * radii, 8 * radii), BF16),
    )
    results = pl.pallas_call(
        functools.partial(kernel, dims),
        out_shape=held,
        in_specs=[pl.BlockSpec(memory_space=pltpu.SMEM)] * 3
        + [pl.BlockSpec(memory_space=pltpu.VMEM)]
        + [anywhere] * 5,
        out_specs=(pl.BlockSpec(memory_space=pltpu.VMEM),) * len(held),
        scratch_shapes=[
            pltpu.VMEM(first_weights.shape[::-1], F32),
            pltpu.VMEM(second_weights.shape[::-1], F32),
            pltpu.VMEM(table.shape, BF16),
            pltpu.VMEM((slots, depth, degrees), BF16),
            pltpu.VMEM((8, 2 * lat, half), BF16),
            pltpu.VMEM((2, 512, half), BF16),
            pltpu.VMEM((pairs, pairs), BF16),
            pltpu.VMEM((512, 4 * pairs), BF16),
            pltpu.VMEM((pairs * 16, 128), F32),
            pltpu.VMEM((tiles, devices, slots, 16, 128), BF16),
            pltpu.VMEM((devices, slots, tiles, 16, 128), BF16),
            pltpu.VMEM((tiles, devices, slots, 16, 128), BF16),
            pltpu.VMEM((devices, slots - 1, tiles, 16, 128), BF16),
            pltpu.SemaphoreType.DMA((2,)),
            pltpu.SemaphoreType.DMA((4, 2, tiles, 2)),
            pltpu.SemaphoreType.DMA((2,)),
            pltpu.SemaphoreType.DMA((slots,)),
            pltpu.SemaphoreType.DMA((3,)),
            pltpu.SemaphoreType.DMA((2,)),
            pltpu.SemaphoreType.DMA((tiles,)),
            pltpu.SemaphoreType.DMA((tiles,)),
            pltpu.SemaphoreType.DMA((len(groups),)),
            pltpu.SemaphoreType.DMA((len(groups),)),
        ],
        compiler_params=pltpu.CompilerParams(
            collective_id=0, has_side_effects=True, vmem_limit_bytes=50 * 2**20
        ),
        cost_estimate=pl.CostEstimate(
            flops=2 * macs, bytes_accessed=2 * (grid_fields.size + legendre.size), transcendentals=0
        ),
    )(
        pair_list,
        stencil_start,
        inv_radius,
        pair_list.reshape(1, pairs),
        first_weights.T,
        second_weights.T,
        grid_fields,
        table,
        legendre,
    )
    out = jax.ShapeDtypeStruct(out_dims, BF16)
    return pl.pallas_call(
        write_kernel,
        out_shape=(out, out),
        in_specs=[pl.BlockSpec(memory_space=pltpu.VMEM)] * len(held),
        out_specs=(anywhere, anywhere),
        scratch_shapes=[
            pltpu.VMEM((3, 2, radii, degrees), BF16),
            pltpu.SemaphoreType.DMA((2, 3, 2)),
            pltpu.SemaphoreType.DMA((3, 2)),
        ],
        compiler_params=pltpu.CompilerParams(vmem_limit_bytes=16 * 2**20),
    )(*[pltpu.with_memory_space_constraint(part, pltpu.VMEM) for part in results])


def solution(mesh):
    in_specs = (P(None, "row", "ma", None), P(), P(("ma", "row"), None, None), P(), P(), P(), P())
    out_specs = (P(None, None, ("ma", "row"), None, None), P(None, None, ("ma", "row"), None, None))
    n_ma, n_row = mesh.shape["ma"], mesh.shape["row"]

    def shards(*args):
        potentials, rad_local, lat, points = args[0].shape
        slots, depth, degrees = args[2].shape
        fits = (
            potentials == 4
            and rad_local == 2
            and lat % 128 == 0
            and depth % 256 == 0
            and degrees % 128 == 0
            and points % 1024 == 0
            and slots == 8
            and n_ma == 4
            and n_row == 8
            and args[1].shape[0] == 256
            and depth == 2 * lat
            and degrees == points // 2
        )
        return (kernel_shards if fits else plain_shards)(*args)

    return jax.shard_map(shards, mesh=mesh, in_specs=in_specs, out_specs=out_specs, check_vma=False)
```

```python
import functools
import math

import jax
import jax.numpy as jnp
import ml_dtypes
import numpy as np
from jax import lax
from jax.experimental import pallas as pl
from jax.experimental.pallas import tpu as pltpu
from jax.sharding import PartitionSpec as P

MESH = pl.DeviceIdType.MESH
F32 = jnp.float32
BF16 = jnp.bfloat16


def degree_table(pair_values, degrees):
    column = jnp.arange(degrees, dtype=jnp.int32)
    upper_side = column[None, :] >= (degrees - pair_values)[:, None]
    degree = jnp.where(upper_side, column[None, :], pair_values[:, None] + column[None, :])
    order_value = jnp.where(upper_side, degrees - pair_values[:, None], pair_values[:, None])
    parity = (degree - order_value) % 2
    return (upper_side.astype(jnp.int32), parity, degree)


def derivative_matrix(stencil_start, weights):
    radius_count, stencil_width = weights.shape
    target = stencil_start[:, None] + jnp.arange(stencil_width, dtype=jnp.int32)[None, :]
    matches = target[:, :, None] == jnp.arange(radius_count, dtype=jnp.int32)[None, None, :]
    return jnp.sum(jnp.where(matches, weights[:, :, None], 0.0), axis=1)


def fourier_table(pair_values, degrees, points):
    orders = jnp.stack([pair_values, degrees - pair_values], axis=1)
    stride = 128
    factor = 1.0 / math.sqrt(points)

    def waves(positions):
        phases = orders[:, :, None] * positions[None, None, :] % points
        angles = phases.astype(jnp.float32) * (2.0 * math.pi / points)
        return jnp.cos(angles), jnp.sin(angles)

    wide_cos, wide_sin = waves(jnp.arange(points // stride, dtype=jnp.int32) * stride)
    fine_cos, fine_sin = waves(jnp.arange(stride, dtype=jnp.int32))
    wide_cos, wide_sin = wide_cos[..., None] * factor, wide_sin[..., None] * factor
    fine_cos, fine_sin = fine_cos[:, :, None, :], fine_sin[:, :, None, :]
    cosine = wide_cos * fine_cos - wide_sin * fine_sin
    sine = wide_sin * fine_cos + wide_cos * fine_sin
    table = jnp.stack([cosine, -sine], axis=2).astype(jnp.bfloat16)
    return table.reshape(pair_values.shape[0], 4, points)


def radial(matrix, values):
    return jnp.einsum("rt,cjtk->cjrk", matrix, values, precision=lax.Precision.HIGHEST)


def curl_parts(poloidal, toroidal, first_matrix, second_matrix, horizontal, inverse):
    poloidal_first = radial(first_matrix, poloidal)
    poloidal_second = radial(second_matrix, poloidal)
    toroidal_first = radial(first_matrix, toroidal)
    radial_part = horizontal * inverse * toroidal
    spheroidal = toroidal_first + inverse * toroidal
    toroidal_part = (
        -(poloidal_second + 2.0 * inverse * poloidal_first)
        + horizontal * inverse * inverse * poloidal
    )
    return jnp.stack([radial_part, spheroidal, toroidal_part], axis=0).astype(jnp.bfloat16)


def select_columns(product, pair_values, degrees):
    upper_side, parity, _ = degree_table(pair_values, degrees)
    wide = (slice(None),) + (None,) * 3 + (slice(None),)
    by_side = jnp.where(upper_side[:, None][wide] == 1, product[:, :, 1], product[:, :, 0])
    return jnp.where(parity[wide] == 1, by_side[:, 1], by_side[:, 0])


def plain_shards(
    grid_fields, pair_list, legendre, stencil_start, first_weights, second_weights, inv_radius
):
    potentials, rad_local, lat_local, points = grid_fields.shape
    degrees = legendre.shape[2]
    slots_here = legendre.shape[0]
    band_count = lax.axis_size("ma")
    rows_axis = lax.axis_size("row")
    fourier = fourier_table(pair_list, degrees, points)
    coefficients = jnp.einsum(
        "jsx,prhx->jsprh", fourier, grid_fields, preferred_element_type=jnp.float32
    ).astype(jnp.bfloat16)
    southern = lax.axis_index("ma") >= band_count // 2
    coefficients = jnp.where(southern, jnp.flip(coefficients, axis=-1), coefficients)
    at_owners = lax.all_to_all(
        coefficients, ("ma", "row"), split_axis=0, concat_axis=0, tiled=True
    ).reshape(band_count, rows_axis, slots_here, 2, 2, potentials, rad_local, lat_local)
    first_slot = (lax.axis_index("ma") * rows_axis + lax.axis_index("row")) * slots_here
    own_pairs = lax.dynamic_slice_in_dim(pair_list, first_slot, slots_here, 0)
    widened = at_owners.astype(jnp.float32)
    north = widened[: band_count // 2]
    south = jnp.flip(widened[band_count // 2 :], axis=0)
    folded = jnp.stack([north + south, north - south], axis=0).astype(jnp.bfloat16)
    folded = jnp.transpose(folded, (3, 0, 4, 5, 6, 2, 7, 1, 8)).reshape(
        slots_here, 8 * potentials * rows_axis * rad_local, -1
    )
    product = jnp.einsum("jmh,jhk->jmk", folded, legendre, preferred_element_type=jnp.float32)
    product = product.reshape(slots_here, 2, 2, 2, potentials, rows_axis * rad_local, degrees)
    chosen = select_columns(product, own_pairs, degrees).astype(jnp.bfloat16)
    spectral = jnp.transpose(chosen, (2, 1, 0, 3, 4))
    degree = degree_table(own_pairs, degrees)[2]
    horizontal = ((degree * (degree + 1)).astype(jnp.float32) / (degrees * degrees))[
        None, :, None, :
    ]
    inverse = inv_radius[:, None]
    first_matrix = derivative_matrix(stencil_start, first_weights)
    second_matrix = derivative_matrix(stencil_start, second_weights)
    widened = spectral.astype(jnp.float32)
    current = curl_parts(widened[0], widened[1], first_matrix, second_matrix, horizontal, inverse)
    vorticity = curl_parts(widened[2], widened[3], first_matrix, second_matrix, horizontal, inverse)
    return (current, vorticity)


def order_table(pairs, degrees, points):
    q = np.arange(pairs)
    orders = np.stack([q, degrees - q], axis=0)
    phase = (orders[:, :, None] * np.arange(points // 2)[None, None, :]) % points
    angle = phase * (2.0 * np.pi / points)
    waves = np.stack([np.cos(angle), -np.sin(angle)], axis=1) / math.sqrt(points)
    waves = waves.reshape(2, 2, pairs // 2, 2, points // 2)
    waves = np.transpose(waves, (3, 0, 1, 2, 4)).reshape(2, 2 * pairs, points // 2)
    waves = np.ascontiguousarray(np.swapaxes(waves, 1, 2))
    return waves.astype(np.float32).astype(ml_dtypes.bfloat16)


def curl(rows, tables, upper, horizontal, matrices):
    half = len(rows) // 2
    total = jnp.dot(
        jnp.concatenate(rows[:half], axis=1), tables[0], preferred_element_type=F32
    ) + jnp.dot(jnp.concatenate(rows[half:], axis=1), tables[1], preferred_element_type=F32)
    count = total.shape[0]
    side = lax.broadcasted_iota(jnp.int32, (count, 1), 0) // 2 % 2
    modes = jnp.where(side == upper, total, 0.0).astype(BF16)
    result = jnp.dot(matrices[0], modes, preferred_element_type=F32) + jnp.dot(
        matrices[1], modes, preferred_element_type=F32
    )
    radii = count // 8
    parts = {}
    for c in (0, 1):
        block = [result[(2 * p + c) * radii : (2 * p + c + 1) * radii] for p in range(4)]
        parts[0, c] = (block[0] * horizontal).astype(BF16)
        parts[1, c] = block[1].astype(BF16)
        parts[2, c] = (block[2] + horizontal * block[3]).astype(BF16)
    return parts


def kernel(
    dims,
    pairs_ref,
    start_ref,
    inverse_ref,
    pair_row_ref,
    first_hbm,
    second_hbm,
    grid_hbm,
    table_hbm,
    legendre_hbm,
    current_ref,
    vorticity_ref,
    last_in,
    last_tables,
    last_rows,
    matrices,
    first_ref,
    second_ref,
    table,
    legendre,
    shared,
    halves,
    chosen,
    orders,
    wide,
    out_a,
    out_b,
    in_a,
    in_b,
    weight_sem,
    grid_sem,
    table_sem,
    legendre_sem,
    own_sem,
    last_sem,
    send_a,
    recv_a,
    send_b,
    recv_b,
):
    n_ma, n_row, slots, lat, half, degrees, pairs, groups = dims
    devices = n_ma * n_row
    tiles = lat // 128
    my_ma, my_row = lax.axis_index("ma"), lax.axis_index("row")
    me = my_ma * n_row + my_row

    def partner(i):
        far = n_row // 2
        mask = i % far + far * (1 - i // (devices // 2)) + n_row * (i % (devices // 2) // far)
        mask = lax.rem(mask, devices)
        place = 0
        bit = 1
        while bit < devices:
            place = place + bit * lax.rem(lax.div(me, bit) + lax.div(mask, bit), 2)
            bit *= 2
        return place

    def partner_of(n):
        return partner(n + n // (devices // 2))

    def mesh_place(place):
        return lax.div(place, n_row), lax.rem(place, n_row)

    barrier = pltpu.get_barrier_semaphore()

    def greet():
        steps = {}
        for name, size, mine in (("ma", n_ma, my_ma), ("row", n_row, my_row)):
            steps[name] = [
                (1 << b) * (1 - 2 * lax.rem(lax.div(mine, 1 << b), 2))
                for b in range(size.bit_length() - 1)
            ]
        for mask in range(devices - 1, 0, -1):
            ma, row = my_ma, my_row
            for b, step in enumerate(steps["row"]):
                row = row + step if mask >> b & 1 else row
            for b, step in enumerate(steps["ma"]):
                ma = ma + step if (mask // n_row) >> b & 1 else ma
            pl.semaphore_signal(barrier, inc=1, device_id=(ma, row), device_id_type=MESH)

    def load_table(e):
        return pltpu.make_async_copy(table_hbm.at[e], table.at[e], table_sem.at[e])

    def load_fields(f, r, t, side):
        return pltpu.make_async_copy(
            grid_hbm.at[f, r, pl.ds(t * 128, 128), pl.ds(side * half, half)],
            shared.at[f * 2 + r, pl.ds(side * lat + t * 128, 128)],
            grid_sem.at[f, r, t, side],
        )

    def load_weights():
        return (
            pltpu.make_async_copy(first_hbm, first_ref, weight_sem.at[0]),
            pltpu.make_async_copy(second_hbm, second_ref, weight_sem.at[1]),
        )

    def load_legendre(j):
        return pltpu.make_async_copy(legendre_hbm.at[j], legendre.at[j], legendre_sem.at[j])

    def start_fields(chunk, t):
        for r in (0, 1):
            for f in (0, 1):
                for side in (0, 1):
                    load_fields(2 * chunk + f, r, t, side).start()

    start_fields(0, 0)
    for e in (0, 1):
        load_table(e).start()
    greet()

    def analyse(chunk, t):
        count = pairs // 2
        for r in (0, 1):
            for f in (0, 1):
                which = 4 * chunk + f * 2 + r
                for side in (0, 1):
                    load_fields(2 * chunk + f, r, t, side).wait()
                for cols in range(0, half, 512):
                    west = shared[which, pl.ds(t * 128, 128), cols : cols + 512]
                    east = shared[which, pl.ds(lat + t * 128, 128), cols : cols + 512]
                    place = (slice((r * 2 + f) * 128, (r * 2 + f + 1) * 128), slice(cols, cols + 512))
                    halves[(0,) + place] = west + east
                    halves[(1,) + place] = west - east
        for e in (0, 1):
            if chunk == 0 and isinstance(t, int) and t == 0:
                load_table(e).wait()
            values = jnp.dot(halves[e], table[e], preferred_element_type=F32).astype(BF16)
            for sc in range(4):
                at = sc * pairs + e * count
                orders[:, at : at + count] = values[:, sc * count : (sc + 1) * count]
        if not (chunk == 0 and isinstance(t, int) and t == 0):
            spread()

    def spread():
        for sc in range(4):
            values = lax.dot_general(
                chosen[...],
                orders[:, sc * pairs : (sc + 1) * pairs],
                (((1,), (1,)), ((), ())),
                preferred_element_type=F32,
            )
            for rf in range(4):
                wide[pl.ds(rf * 4 + sc, pairs, stride=16), :] = values[
                    :, rf * 128 : (rf + 1) * 128
                ]

    def spread_half(far):
        height = n_row // 2 * slots
        side = my_row // (n_row // 2)
        side = 1 - side if far else side
        starts = [pl.multiple_of((2 * a + side) * height, height) for a in range(n_ma)]
        some = jnp.concatenate([chosen[pl.ds(start, height), :] for start in starts], axis=0)
        for sc in range(4):
            values = lax.dot_general(
                some,
                orders[:, sc * pairs : (sc + 1) * pairs],
                (((1,), (1,)), ((), ())),
                preferred_element_type=F32,
            )
            for rf in range(4):
                for a, start in enumerate(starts):
                    wide[pl.ds(start * 16 + rf * 4 + sc, height, stride=16), :] = values[
                        a * height : (a + 1) * height, rf * 128 : (rf + 1) * 128
                    ]

    def pick(chunk, t, who):
        rows = pl.ds(pl.multiple_of(who * (slots * 16), slots * 16), slots * 16)
        values = wide[rows, :].astype(BF16).reshape(slots, 16, 128)
        if chunk == 0:
            out_a[t, who] = values
        else:
            out_b[who, :, t] = values

    def copy_a(t, place):
        return pltpu.make_async_remote_copy(
            src_ref=out_a.at[t, place],
            dst_ref=in_a.at[t, me],
            send_sem=send_a.at[t],
            recv_sem=recv_a.at[t],
            device_id=mesh_place(place),
            device_id_type=MESH,
        )

    last = slots - 1

    def ends_b(g, source, target):
        if g == len(groups) - 1:
            return out_b.at[source, last], last_in.at[target]
        part = pl.ds(*groups[g])
        return out_b.at[source, part], in_b.at[target, part]

    def copy_b(g, place):
        source, target = ends_b(g, place, me)
        return pltpu.make_async_remote_copy(
            src_ref=source,
            dst_ref=target,
            send_sem=send_b.at[g],
            recv_sem=recv_b.at[g],
            device_id=mesh_place(place),
            device_id_type=MESH,
        )

    def copy_own(chunk):
        if chunk == 0:
            pairs_of_refs = [(out_a.at[:, me], in_a.at[:, me])]
        else:
            pairs_of_refs = [
                (out_b.at[me, pl.ds(0, last)], in_b.at[me]),
                (out_b.at[me, last], last_in.at[me]),
            ]
        return [
            pltpu.make_async_copy(source, target, own_sem.at[chunk + n])
            for n, (source, target) in enumerate(pairs_of_refs)
        ]

    def all_a(t, sem):
        some = pl.ds(0, devices - 1)
        pltpu.make_async_copy(out_a.at[t, some], in_a.at[t, some], sem).wait()

    def all_b(g, sem):
        some = pl.ds(0, devices - 1)
        pltpu.make_async_copy(*ends_b(g, some, some), sem).wait()

    kind = lax.broadcasted_iota(jnp.int32, (pairs, 1), 0)
    kind = jnp.where(kind < pairs // 2, 2 * kind, 2 * kind - pairs + 1)
    by_order = jnp.where(kind == pair_row_ref[...], 1.0, 0.0).astype(F32)
    chosen[...] = by_order.T.astype(BF16)

    for t in range(tiles):
        analyse(0, t)
        if t == 0:
            for later in range(1, tiles):
                start_fields(0, later)
            for later in range(tiles):
                start_fields(1, later)
            pl.semaphore_wait(barrier, devices - 1)

        def send_tile(n, _):
            place = partner_of(n)
            pick(0, t, place)
            copy_a(t, place).start()
            return 0

        if t == 0:
            spread_half(True)
            lax.fori_loop(0, devices // 2, send_tile, 0)
            spread_half(False)
            lax.fori_loop(devices // 2, devices - 1, send_tile, 0)
        else:
            lax.fori_loop(0, devices - 1, send_tile, 0)
        pick(0, t, me)
    for copy in copy_own(0):
        copy.start()
    for j in range(slots):
        load_legendre(j).start()
    for copy in load_weights():
        copy.start()

    def second_chunk(t, _):
        analyse(1, t)

        def one(who, _):
            pick(1, t, who)
            return 0

        lax.fori_loop(0, devices, one, 0)
        return 0

    lax.fori_loop(0, tiles, second_chunk, 0)
    for g in range(len(groups)):

        def send_group(n, _):
            copy_b(g, partner_of(n)).start()
            return 0

        lax.fori_loop(0, devices - 1, send_group, 0)
    for copy in copy_own(1):
        copy.start()

    for copy in load_weights():
        copy.wait()
    radii = n_row * 2
    out_row = lax.broadcasted_iota(jnp.int32, (8 * radii, 1), 0)
    in_row = lax.broadcasted_iota(jnp.int32, (1, 8 * radii), 1)
    of_part, of_radius = out_row // (2 * radii), out_row % radii
    at_radius = in_row // 8

    def add_radius(r, held):
        start, inverse = held
        here = of_radius == r
        return jnp.where(here, start_ref[r], start), jnp.where(here, inverse_ref[r], inverse)

    start, inverse = lax.fori_loop(
        0,
        radii,
        add_radius,
        (jnp.zeros((8 * radii, 1), jnp.int32), jnp.zeros((8 * radii, 1), F32)),
    )
    lane = lax.broadcasted_iota(jnp.int32, (1, radii), 1)

    def per_row(values):
        return jnp.sum(jnp.where(lane == of_radius, values, 0.0), axis=1, keepdims=True)

    first_matrix = jnp.zeros((8 * radii, 8 * radii), F32)
    second_matrix = first_matrix
    for w in range(first_ref.shape[0]):
        here = at_radius == start + w
        first_matrix += jnp.where(here, per_row(first_ref[w : w + 1, :]), 0.0)
        second_matrix += jnp.where(here, per_row(second_ref[w : w + 1, :]), 0.0)
    diagonal = jnp.where(of_radius == at_radius, inverse, 0.0)
    matrix = jnp.where(
        of_part < 2,
        diagonal + jnp.where(of_part == 1, first_matrix, 0.0),
        jnp.where(
            of_part == 2, -(second_matrix + 2.0 * inverse * first_matrix), diagonal * inverse
        ),
    )
    joined = ((in_row // 4) % 2 == jnp.where(of_part < 2, 1, 0)) & (
        in_row % 2 == (out_row // radii) % 2
    )
    matrix = jnp.where(joined, matrix, 0.0)
    matrix_high = matrix.astype(BF16)
    matrices[0] = matrix_high
    matrices[1] = (matrix - matrix_high.astype(F32)).astype(BF16)
    column = lax.broadcasted_iota(jnp.int32, (1, degrees), 1)
    depth = legendre.shape[1]

    def of_slot(j):
        q = pairs_ref[me * slots + j]
        upper = column >= degrees - q
        order = jnp.where(upper, degrees - q, q)
        degree = jnp.where(upper, column, q + column)
        sign = 1.0 - 2.0 * ((degree - order) % 2).astype(F32)
        horizontal = (degree * (degree + 1)).astype(F32) / (degrees * degrees)
        return upper.astype(jnp.int32), sign, horizontal

    def mirror(j, _):
        load_legendre(j).wait()
        sign = of_slot(j)[1]
        block = 256
        turn = (
            lax.broadcasted_iota(jnp.int32, (block, block), 0)
            + lax.broadcasted_iota(jnp.int32, (block, block), 1)
            == block - 1
        )
        turn = jnp.where(turn, 1.0, 0.0).astype(BF16)
        for b in range(depth // block):
            low = depth - (b + 1) * block
            values = jnp.dot(turn, legendre[j, low : low + block, :], preferred_element_type=F32)
            shared[j, b * block : (b + 1) * block, :] = (values * sign).astype(BF16)
        return 0

    lax.fori_loop(0, slots, mirror, 0)
    last_copies = [
        pltpu.make_async_copy(part.at[last], last_tables.at[n], last_sem.at[n])
        for n, part in enumerate((legendre, shared))
    ]
    for copy in last_copies:
        copy.start()
    upper, _, horizontal = of_slot(last)
    last_rows[0] = upper.astype(F32)
    last_rows[1] = horizontal

    def transform(chunk, j):
        upper, _, horizontal = of_slot(j)
        rows = [
            (
                in_a[t, a * n_row : (a + 1) * n_row, j]
                if chunk == 0
                else in_b[a * n_row : (a + 1) * n_row, j, t]
            ).reshape(n_row * 16, 128)
            for a in range(n_ma)
            for t in range(tiles)
        ]
        parts = curl(rows, (legendre[j], shared[j]), upper, horizontal, matrices)
        for (part, c), values in parts.items():
            (current_ref, vorticity_ref)[chunk][part, c, j] = values

    for t in range(tiles):
        all_a(t, recv_a.at[t])
    for copy in copy_own(0):
        copy.wait()

    def first(j, _):
        transform(0, j)
        return 0

    lax.fori_loop(0, slots, first, 0)
    for copy in copy_own(1):
        copy.wait()
    for t in range(tiles):
        all_a(t, send_a.at[t])
    for g in range(len(groups)):
        if g > 0:
            all_b(g - 1, send_b.at[g - 1])
        all_b(g, recv_b.at[g])

        def second(k, _):
            transform(1, groups[g][0] + k)
            return 0

        if g < len(groups) - 1:
            lax.fori_loop(0, groups[g][1], second, 0)
        if g == 0:
            for copy in last_copies:
                copy.wait()
    all_b(len(groups) - 1, send_b.at[len(groups) - 1])


def write_kernel(
    current, vorticity, last_in, last_tables, last_rows, matrices, current_hbm, vorticity_hbm,
    staged, sem, last_sem,
):
    last = vorticity.shape[2] - 1
    copies = []
    for part in range(3):
        for c in (0, 1):
            copies.append(
                pltpu.make_async_copy(
                    vorticity.at[part, c, pl.ds(0, last)],
                    vorticity_hbm.at[part, c, pl.ds(0, last)],
                    sem.at[0, part, c],
                )
            )
            copies.append(
                pltpu.make_async_copy(
                    current.at[part, c], current_hbm.at[part, c], sem.at[1, part, c]
                )
            )
    for copy in copies:
        copy.start()
    bands, count = 4, last_in.shape[0] // 4
    rows = [
        last_in[a * count : (a + 1) * count, t].reshape(count * 16, 128)
        for a in range(bands)
        for t in range(last_in.shape[1])
    ]
    width = staged.shape[3] // 2
    for h in (0, 1):
        columns = slice(h * width, (h + 1) * width)
        parts = curl(
            rows,
            (last_tables[0, :, columns], last_tables[1, :, columns]),
            last_rows[0, :, columns].astype(jnp.int32),
            last_rows[1, :, columns],
            matrices,
        )
        for (part, c), values in parts.items():
            staged[part, c, :, columns] = values
            copy = pltpu.make_async_copy(
                staged.at[part, c, :, columns],
                vorticity_hbm.at[part, c, last, :, columns],
                last_sem.at[h, part, c],
            )
            copy.start()
            copies.append(copy)
    for copy in copies:
        copy.wait()


def kernel_shards(
    grid_fields, pair_list, legendre, stencil_start, first_weights, second_weights, inv_radius
):
    _, _, lat, points = grid_fields.shape
    slots, depth, degrees = legendre.shape
    n_ma, n_row = lax.axis_size("ma"), lax.axis_size("row")
    devices = n_ma * n_row
    pairs = pair_list.shape[0]
    radii = 2 * n_row
    tiles = lat // 128
    half = points // 2
    groups = [(0, slots // 2), (slots // 2, slots // 2 - 1), (slots - 1, 1)]
    table = jnp.asarray(order_table(pairs, degrees, points))
    out_dims = (3, 2, slots, radii, degrees)
    anywhere = pl.BlockSpec(memory_space=pl.ANY)
    dims = (n_ma, n_row, slots, lat, half, degrees, pairs, groups)
    macs = 8 * lat * half * pairs * 4 + 2 * slots * 128 * 2 * depth * degrees
    held = (
        pltpu.VMEM(out_dims, BF16),
        pltpu.VMEM(out_dims, BF16),
        pltpu.VMEM((devices, tiles, 16, 128), BF16),
        pltpu.VMEM((2, depth, degrees), BF16),
        pltpu.VMEM((2, 1, degrees), F32),
        pltpu.VMEM((2, 8 * radii, 8 * radii), BF16),
    )
    results = pl.pallas_call(
        functools.partial(kernel, dims),
        out_shape=held,
        in_specs=[pl.BlockSpec(memory_space=pltpu.SMEM)] * 3
        + [pl.BlockSpec(memory_space=pltpu.VMEM)]
        + [anywhere] * 5,
        out_specs=(pl.BlockSpec(memory_space=pltpu.VMEM),) * len(held),
        scratch_shapes=[
            pltpu.VMEM(first_weights.shape[::-1], F32),
            pltpu.VMEM(second_weights.shape[::-1], F32),
            pltpu.VMEM(table.shape, BF16),
            pltpu.VMEM((slots, depth, degrees), BF16),
            pltpu.VMEM((8, 2 * lat, half), BF16),
            pltpu.VMEM((2, 512, half), BF16),
            pltpu.VMEM((pairs, pairs), BF16),
            pltpu.VMEM((512, 4 * pairs), BF16),
            pltpu.VMEM((pairs * 16, 128), F32),
            pltpu.VMEM((tiles, devices, slots, 16, 128), BF16),
            pltpu.VMEM((devices, slots, tiles, 16, 128), BF16),
            pltpu.VMEM((tiles, devices, slots, 16, 128), BF16),
            pltpu.VMEM((devices, slots - 1, tiles, 16, 128), BF16),
            pltpu.SemaphoreType.DMA((2,)),
            pltpu.SemaphoreType.DMA((4, 2, tiles, 2)),
            pltpu.SemaphoreType.DMA((2,)),
            pltpu.SemaphoreType.DMA((slots,)),
            pltpu.SemaphoreType.DMA((3,)),
            pltpu.SemaphoreType.DMA((2,)),
            pltpu.SemaphoreType.DMA((tiles,)),
            pltpu.SemaphoreType.DMA((tiles,)),
            pltpu.SemaphoreType.DMA((len(groups),)),
            pltpu.SemaphoreType.DMA((len(groups),)),
        ],
        compiler_params=pltpu.CompilerParams(
            collective_id=0, has_side_effects=True, vmem_limit_bytes=50 * 2**20
        ),
        cost_estimate=pl.CostEstimate(
            flops=2 * macs, bytes_accessed=2 * (grid_fields.size + legendre.size), transcendentals=0
        ),
    )(
        pair_list,
        stencil_start,
        inv_radius,
        pair_list.reshape(1, pairs),
        first_weights.T,
        second_weights.T,
        grid_fields,
        table,
        legendre,
    )
    out = jax.ShapeDtypeStruct(out_dims, BF16)
    return pl.pallas_call(
        write_kernel,
        out_shape=(out, out),
        in_specs=[pl.BlockSpec(memory_space=pltpu.VMEM)] * len(held),
        out_specs=(anywhere, anywhere),
        scratch_shapes=[
            pltpu.VMEM((3, 2, radii, degrees), BF16),
            pltpu.SemaphoreType.DMA((2, 3, 2)),
            pltpu.SemaphoreType.DMA((2, 3, 2)),
        ],
        compiler_params=pltpu.CompilerParams(vmem_limit_bytes=16 * 2**20),
    )(*[pltpu.with_memory_space_constraint(part, pltpu.VMEM) for part in results])


def solution(mesh):
    in_specs = (P(None, "row", "ma", None), P(), P(("ma", "row"), None, None), P(), P(), P(), P())
    out_specs = (P(None, None, ("ma", "row"), None, None), P(None, None, ("ma", "row"), None, None))
    n_ma, n_row = mesh.shape["ma"], mesh.shape["row"]

    def shards(*args):
        potentials, rad_local, lat, points = args[0].shape
        slots, depth, degrees = args[2].shape
        fits = (
            potentials == 4
            and rad_local == 2
            and lat % 128 == 0
            and depth % 256 == 0
            and degrees % 128 == 0
            and points % 1024 == 0
            and slots == 8
            and n_ma == 4
            and n_row == 8
            and args[1].shape[0] == 256
            and depth == 2 * lat
            and degrees == points // 2
        )
        return (kernel_shards if fits else plain_shards)(*args)

    return jax.shard_map(shards, mesh=mesh, in_specs=in_specs, out_specs=out_specs, check_vma=False)
```

```python
import functools
import math

import jax
import jax.numpy as jnp
import ml_dtypes
import numpy as np
from jax import lax
from jax.experimental import pallas as pl
from jax.experimental.pallas import tpu as pltpu
from jax.sharding import PartitionSpec as P

MESH = pl.DeviceIdType.MESH
F32 = jnp.float32
BF16 = jnp.bfloat16


def degree_table(pair_values, degrees):
    column = jnp.arange(degrees, dtype=jnp.int32)
    upper_side = column[None, :] >= (degrees - pair_values)[:, None]
    degree = jnp.where(upper_side, column[None, :], pair_values[:, None] + column[None, :])
    order_value = jnp.where(upper_side, degrees - pair_values[:, None], pair_values[:, None])
    parity = (degree - order_value) % 2
    return (upper_side.astype(jnp.int32), parity, degree)


def derivative_matrix(stencil_start, weights):
    radius_count, stencil_width = weights.shape
    target = stencil_start[:, None] + jnp.arange(stencil_width, dtype=jnp.int32)[None, :]
    matches = target[:, :, None] == jnp.arange(radius_count, dtype=jnp.int32)[None, None, :]
    return jnp.sum(jnp.where(matches, weights[:, :, None], 0.0), axis=1)


def fourier_table(pair_values, degrees, points):
    orders = jnp.stack([pair_values, degrees - pair_values], axis=1)
    stride = 128
    factor = 1.0 / math.sqrt(points)

    def waves(positions):
        phases = orders[:, :, None] * positions[None, None, :] % points
        angles = phases.astype(jnp.float32) * (2.0 * math.pi / points)
        return jnp.cos(angles), jnp.sin(angles)

    wide_cos, wide_sin = waves(jnp.arange(points // stride, dtype=jnp.int32) * stride)
    fine_cos, fine_sin = waves(jnp.arange(stride, dtype=jnp.int32))
    wide_cos, wide_sin = wide_cos[..., None] * factor, wide_sin[..., None] * factor
    fine_cos, fine_sin = fine_cos[:, :, None, :], fine_sin[:, :, None, :]
    cosine = wide_cos * fine_cos - wide_sin * fine_sin
    sine = wide_sin * fine_cos + wide_cos * fine_sin
    table = jnp.stack([cosine, -sine], axis=2).astype(jnp.bfloat16)
    return table.reshape(pair_values.shape[0], 4, points)


def radial(matrix, values):
    return jnp.einsum("rt,cjtk->cjrk", matrix, values, precision=lax.Precision.HIGHEST)


def curl_parts(poloidal, toroidal, first_matrix, second_matrix, horizontal, inverse):
    poloidal_first = radial(first_matrix, poloidal)
    poloidal_second = radial(second_matrix, poloidal)
    toroidal_first = radial(first_matrix, toroidal)
    radial_part = horizontal * inverse * toroidal
    spheroidal = toroidal_first + inverse * toroidal
    toroidal_part = (
        -(poloidal_second + 2.0 * inverse * poloidal_first)
        + horizontal * inverse * inverse * poloidal
    )
    return jnp.stack([radial_part, spheroidal, toroidal_part], axis=0).astype(jnp.bfloat16)


def select_columns(product, pair_values, degrees):
    upper_side, parity, _ = degree_table(pair_values, degrees)
    wide = (slice(None),) + (None,) * 3 + (slice(None),)
    by_side = jnp.where(upper_side[:, None][wide] == 1, product[:, :, 1], product[:, :, 0])
    return jnp.where(parity[wide] == 1, by_side[:, 1], by_side[:, 0])


def plain_shards(
    grid_fields, pair_list, legendre, stencil_start, first_weights, second_weights, inv_radius
):
    potentials, rad_local, lat_local, points = grid_fields.shape
    degrees = legendre.shape[2]
    slots_here = legendre.shape[0]
    band_count = lax.axis_size("ma")
    rows_axis = lax.axis_size("row")
    fourier = fourier_table(pair_list, degrees, points)
    coefficients = jnp.einsum(
        "jsx,prhx->jsprh", fourier, grid_fields, preferred_element_type=jnp.float32
    ).astype(jnp.bfloat16)
    southern = lax.axis_index("ma") >= band_count // 2
    coefficients = jnp.where(southern, jnp.flip(coefficients, axis=-1), coefficients)
    at_owners = lax.all_to_all(
        coefficients, ("ma", "row"), split_axis=0, concat_axis=0, tiled=True
    ).reshape(band_count, rows_axis, slots_here, 2, 2, potentials, rad_local, lat_local)
    first_slot = (lax.axis_index("ma") * rows_axis + lax.axis_index("row")) * slots_here
    own_pairs = lax.dynamic_slice_in_dim(pair_list, first_slot, slots_here, 0)
    widened = at_owners.astype(jnp.float32)
    north = widened[: band_count // 2]
    south = jnp.flip(widened[band_count // 2 :], axis=0)
    folded = jnp.stack([north + south, north - south], axis=0).astype(jnp.bfloat16)
    folded = jnp.transpose(folded, (3, 0, 4, 5, 6, 2, 7, 1, 8)).reshape(
        slots_here, 8 * potentials * rows_axis * rad_local, -1
    )
    product = jnp.einsum("jmh,jhk->jmk", folded, legendre, preferred_element_type=jnp.float32)
    product = product.reshape(slots_here, 2, 2, 2, potentials, rows_axis * rad_local, degrees)
    chosen = select_columns(product, own_pairs, degrees).astype(jnp.bfloat16)
    spectral = jnp.transpose(chosen, (2, 1, 0, 3, 4))
    degree = degree_table(own_pairs, degrees)[2]
    horizontal = ((degree * (degree + 1)).astype(jnp.float32) / (degrees * degrees))[
        None, :, None, :
    ]
    inverse = inv_radius[:, None]
    first_matrix = derivative_matrix(stencil_start, first_weights)
    second_matrix = derivative_matrix(stencil_start, second_weights)
    widened = spectral.astype(jnp.float32)
    current = curl_parts(widened[0], widened[1], first_matrix, second_matrix, horizontal, inverse)
    vorticity = curl_parts(widened[2], widened[3], first_matrix, second_matrix, horizontal, inverse)
    return (current, vorticity)


def order_table(pairs, degrees, points):
    q = np.arange(pairs)
    orders = np.stack([q, degrees - q], axis=0)
    phase = (orders[:, :, None] * np.arange(points // 2)[None, None, :]) % points
    angle = phase * (2.0 * np.pi / points)
    waves = np.stack([np.cos(angle), -np.sin(angle)], axis=1) / math.sqrt(points)
    waves = waves.reshape(2, 2, pairs // 2, 2, points // 2)
    waves = np.transpose(waves, (3, 0, 1, 2, 4)).reshape(2, 2 * pairs, points // 2)
    waves = np.ascontiguousarray(np.swapaxes(waves, 1, 2))
    return waves.astype(np.float32).astype(ml_dtypes.bfloat16)


def curl(rows, tables, upper, horizontal, matrices):
    half = len(rows) // 2
    total = jnp.dot(
        jnp.concatenate(rows[:half], axis=1), tables[0], preferred_element_type=F32
    ) + jnp.dot(jnp.concatenate(rows[half:], axis=1), tables[1], preferred_element_type=F32)
    count = total.shape[0]
    side = lax.broadcasted_iota(jnp.int32, (count, 1), 0) // 2 % 2
    modes = jnp.where(side == upper, total, 0.0).astype(BF16)
    result = jnp.dot(matrices[0], modes, preferred_element_type=F32) + jnp.dot(
        matrices[1], modes, preferred_element_type=F32
    )
    radii = count // 8
    parts = {}
    for c in (0, 1):
        block = [result[(2 * p + c) * radii : (2 * p + c + 1) * radii] for p in range(4)]
        parts[0, c] = (block[0] * horizontal).astype(BF16)
        parts[1, c] = block[1].astype(BF16)
        parts[2, c] = (block[2] + horizontal * block[3]).astype(BF16)
    return parts


def kernel(
    dims,
    pairs_ref,
    start_ref,
    inverse_ref,
    pair_row_ref,
    first_hbm,
    second_hbm,
    grid_hbm,
    table_hbm,
    legendre_hbm,
    current_ref,
    vorticity_ref,
    last_in,
    last_tables,
    last_rows,
    matrices,
    first_ref,
    second_ref,
    table,
    legendre,
    shared,
    halves,
    chosen,
    orders,
    wide,
    out_a,
    out_b,
    in_a,
    in_b,
    weight_sem,
    grid_sem,
    table_sem,
    legendre_sem,
    own_sem,
    last_sem,
    send_a,
    recv_a,
    send_b,
    recv_b,
):
    n_ma, n_row, slots, lat, half, degrees, pairs, groups = dims
    devices = n_ma * n_row
    tiles = lat // 128
    my_ma, my_row = lax.axis_index("ma"), lax.axis_index("row")
    me = my_ma * n_row + my_row

    def partner(i):
        far = n_row // 2
        mask = i % far + far * (1 - i // (devices // 2)) + n_row * (i % (devices // 2) // far)
        mask = lax.rem(mask, devices)
        place = 0
        bit = 1
        while bit < devices:
            place = place + bit * lax.rem(lax.div(me, bit) + lax.div(mask, bit), 2)
            bit *= 2
        return place

    def partner_of(n):
        return partner(n + n // (devices // 2))

    def mesh_place(place):
        return lax.div(place, n_row), lax.rem(place, n_row)

    barrier = pltpu.get_barrier_semaphore()

    def greet():
        steps = {}
        for name, size, mine in (("ma", n_ma, my_ma), ("row", n_row, my_row)):
            steps[name] = [
                (1 << b) * (1 - 2 * lax.rem(lax.div(mine, 1 << b), 2))
                for b in range(size.bit_length() - 1)
            ]
        for mask in range(devices - 1, 0, -1):
            ma, row = my_ma, my_row
            for b, step in enumerate(steps["row"]):
                row = row + step if mask >> b & 1 else row
            for b, step in enumerate(steps["ma"]):
                ma = ma + step if (mask // n_row) >> b & 1 else ma
            pl.semaphore_signal(barrier, inc=1, device_id=(ma, row), device_id_type=MESH)

    def load_table(e):
        return pltpu.make_async_copy(table_hbm.at[e], table.at[e], table_sem.at[e])

    def load_fields(f, r, t, side):
        return pltpu.make_async_copy(
            grid_hbm.at[f, r, pl.ds(t * 128, 128), pl.ds(side * half, half)],
            shared.at[f * 2 + r, pl.ds(side * lat + t * 128, 128)],
            grid_sem.at[f, r, t, side],
        )

    def load_weights():
        return (
            pltpu.make_async_copy(first_hbm, first_ref, weight_sem.at[0]),
            pltpu.make_async_copy(second_hbm, second_ref, weight_sem.at[1]),
        )

    def load_legendre(j):
        return pltpu.make_async_copy(legendre_hbm.at[j], legendre.at[j], legendre_sem.at[j])

    def start_fields(chunk, t):
        for r in (0, 1):
            for f in (0, 1):
                for side in (0, 1):
                    load_fields(2 * chunk + f, r, t, side).start()

    start_fields(0, 0)
    for e in (0, 1):
        load_table(e).start()
    greet()

    def analyse(chunk, t):
        count = pairs // 2
        for r in (0, 1):
            for f in (0, 1):
                which = 4 * chunk + f * 2 + r
                for side in (0, 1):
                    load_fields(2 * chunk + f, r, t, side).wait()
                for cols in range(0, half, 512):
                    west = shared[which, pl.ds(t * 128, 128), cols : cols + 512]
                    east = shared[which, pl.ds(lat + t * 128, 128), cols : cols + 512]
                    place = (slice((r * 2 + f) * 128, (r * 2 + f + 1) * 128), slice(cols, cols + 512))
                    halves[(0,) + place] = west + east
                    halves[(1,) + place] = west - east
        for e in (0, 1):
            if chunk == 0 and isinstance(t, int) and t == 0:
                load_table(e).wait()
            values = jnp.dot(halves[e], table[e], preferred_element_type=F32).astype(BF16)
            for sc in range(4):
                at = sc * pairs + e * count
                orders[:, at : at + count] = values[:, sc * count : (sc + 1) * count]
        if not (chunk == 0 and isinstance(t, int) and t == 0):
            spread()

    def spread():
        for sc in range(4):
            values = lax.dot_general(
                chosen[...],
                orders[:, sc * pairs : (sc + 1) * pairs],
                (((1,), (1,)), ((), ())),
                preferred_element_type=F32,
            )
            for rf in range(4):
                wide[pl.ds(rf * 4 + sc, pairs, stride=16), :] = values[
                    :, rf * 128 : (rf + 1) * 128
                ]

    def spread_half(far):
        height = n_row // 2 * slots
        side = my_row // (n_row // 2)
        side = 1 - side if far else side
        starts = [pl.multiple_of((2 * a + side) * height, height) for a in range(n_ma)]
        some = jnp.concatenate([chosen[pl.ds(start, height), :] for start in starts], axis=0)
        for sc in range(4):
            values = lax.dot_general(
                some,
                orders[:, sc * pairs : (sc + 1) * pairs],
                (((1,), (1,)), ((), ())),
                preferred_element_type=F32,
            )
            for rf in range(4):
                for a, start in enumerate(starts):
                    wide[pl.ds(start * 16 + rf * 4 + sc, height, stride=16), :] = values[
                        a * height : (a + 1) * height, rf * 128 : (rf + 1) * 128
                    ]

    def pick(chunk, t, who):
        rows = pl.ds(pl.multiple_of(who * (slots * 16), slots * 16), slots * 16)
        values = wide[rows, :].astype(BF16).reshape(slots, 16, 128)
        if chunk == 0:
            out_a[t, who] = values
        else:
            out_b[who, :, t] = values

    def copy_a(t, place):
        return pltpu.make_async_remote_copy(
            src_ref=out_a.at[t, place],
            dst_ref=in_a.at[t, me],
            send_sem=send_a.at[t],
            recv_sem=recv_a.at[t],
            device_id=mesh_place(place),
            device_id_type=MESH,
        )

    last = slots - 1

    def ends_b(g, source, target):
        if g == len(groups) - 1:
            return out_b.at[source, last], last_in.at[target]
        part = pl.ds(*groups[g])
        return out_b.at[source, part], in_b.at[target, part]

    def copy_b(g, place):
        source, target = ends_b(g, place, me)
        return pltpu.make_async_remote_copy(
            src_ref=source,
            dst_ref=target,
            send_sem=send_b.at[g],
            recv_sem=recv_b.at[g],
            device_id=mesh_place(place),
            device_id_type=MESH,
        )

    def copy_own(chunk):
        if chunk == 0:
            pairs_of_refs = [(out_a.at[:, me], in_a.at[:, me])]
        else:
            pairs_of_refs = [
                (out_b.at[me, pl.ds(0, last)], in_b.at[me]),
                (out_b.at[me, last], last_in.at[me]),
            ]
        return [
            pltpu.make_async_copy(source, target, own_sem.at[chunk + n])
            for n, (source, target) in enumerate(pairs_of_refs)
        ]

    def all_a(t, sem):
        some = pl.ds(0, devices - 1)
        pltpu.make_async_copy(out_a.at[t, some], in_a.at[t, some], sem).wait()

    def all_b(g, sem):
        some = pl.ds(0, devices - 1)
        pltpu.make_async_copy(*ends_b(g, some, some), sem).wait()

    kind = lax.broadcasted_iota(jnp.int32, (pairs, 1), 0)
    kind = jnp.where(kind < pairs // 2, 2 * kind, 2 * kind - pairs + 1)
    by_order = jnp.where(kind == pair_row_ref[...], 1.0, 0.0).astype(F32)
    chosen[...] = by_order.T.astype(BF16)

    for t in range(tiles):
        analyse(0, t)
        if t == 0:
            for later in range(1, tiles):
                start_fields(0, later)
            for later in range(tiles):
                start_fields(1, later)
            pl.semaphore_wait(barrier, devices - 1)

        def send_tile(n, _):
            place = partner_of(n)
            pick(0, t, place)
            copy_a(t, place).start()
            return 0

        if t == 0:
            spread_half(True)
            lax.fori_loop(0, devices // 2, send_tile, 0)
            spread_half(False)
            lax.fori_loop(devices // 2, devices - 1, send_tile, 0)
        else:
            lax.fori_loop(0, devices - 1, send_tile, 0)
        pick(0, t, me)
    for copy in copy_own(0):
        copy.start()
    for j in range(slots):
        load_legendre(j).start()
    for copy in load_weights():
        copy.start()

    def second_chunk(t, _):
        analyse(1, t)

        def one(who, _):
            pick(1, t, who)
            return 0

        lax.fori_loop(0, devices, one, 0)
        return 0

    lax.fori_loop(0, tiles, second_chunk, 0)
    for g in range(len(groups)):

        def send_group(n, _):
            copy_b(g, partner_of(n)).start()
            return 0

        lax.fori_loop(0, devices - 1, send_group, 0)
    for copy in copy_own(1):
        copy.start()

    for copy in load_weights():
        copy.wait()
    radii = n_row * 2
    out_row = lax.broadcasted_iota(jnp.int32, (8 * radii, 1), 0)
    in_row = lax.broadcasted_iota(jnp.int32, (1, 8 * radii), 1)
    of_part, of_radius = out_row // (2 * radii), out_row % radii
    at_radius = in_row // 8

    def add_radius(r, held):
        start, inverse = held
        here = of_radius == r
        return jnp.where(here, start_ref[r], start), jnp.where(here, inverse_ref[r], inverse)

    start, inverse = lax.fori_loop(
        0,
        radii,
        add_radius,
        (jnp.zeros((8 * radii, 1), jnp.int32), jnp.zeros((8 * radii, 1), F32)),
    )
    lane = lax.broadcasted_iota(jnp.int32, (1, radii), 1)

    def per_row(values):
        return jnp.sum(jnp.where(lane == of_radius, values, 0.0), axis=1, keepdims=True)

    first_matrix = jnp.zeros((8 * radii, 8 * radii), F32)
    second_matrix = first_matrix
    for w in range(first_ref.shape[0]):
        here = at_radius == start + w
        first_matrix += jnp.where(here, per_row(first_ref[w : w + 1, :]), 0.0)
        second_matrix += jnp.where(here, per_row(second_ref[w : w + 1, :]), 0.0)
    diagonal = jnp.where(of_radius == at_radius, inverse, 0.0)
    matrix = jnp.where(
        of_part < 2,
        diagonal + jnp.where(of_part == 1, first_matrix, 0.0),
        jnp.where(
            of_part == 2, -(second_matrix + 2.0 * inverse * first_matrix), diagonal * inverse
        ),
    )
    joined = ((in_row // 4) % 2 == jnp.where(of_part < 2, 1, 0)) & (
        in_row % 2 == (out_row // radii) % 2
    )
    matrix = jnp.where(joined, matrix, 0.0)
    matrix_high = matrix.astype(BF16)
    matrices[0] = matrix_high
    matrices[1] = (matrix - matrix_high.astype(F32)).astype(BF16)
    column = lax.broadcasted_iota(jnp.int32, (1, degrees), 1)
    depth = legendre.shape[1]

    def of_slot(j):
        q = pairs_ref[me * slots + j]
        upper = column >= degrees - q
        order = jnp.where(upper, degrees - q, q)
        degree = jnp.where(upper, column, q + column)
        sign = 1.0 - 2.0 * ((degree - order) % 2).astype(F32)
        horizontal = (degree * (degree + 1)).astype(F32) / (degrees * degrees)
        return upper.astype(jnp.int32), sign, horizontal

    def mirror(j, _):
        load_legendre(j).wait()
        sign = of_slot(j)[1]
        block = 256
        turn = (
            lax.broadcasted_iota(jnp.int32, (block, block), 0)
            + lax.broadcasted_iota(jnp.int32, (block, block), 1)
            == block - 1
        )
        turn = jnp.where(turn, 1.0, 0.0).astype(BF16)
        for b in range(depth // block):
            low = depth - (b + 1) * block
            values = jnp.dot(turn, legendre[j, low : low + block, :], preferred_element_type=F32)
            shared[j, b * block : (b + 1) * block, :] = (values * sign).astype(BF16)
        return 0

    lax.fori_loop(0, slots, mirror, 0)
    last_copies = [
        pltpu.make_async_copy(part.at[last], last_tables.at[n], last_sem.at[n])
        for n, part in enumerate((legendre, shared))
    ]
    for copy in last_copies:
        copy.start()
    upper, _, horizontal = of_slot(last)
    last_rows[0] = upper.astype(F32)
    last_rows[1] = horizontal

    def transform(chunk, j):
        upper, _, horizontal = of_slot(j)
        rows = [
            (
                in_a[t, a * n_row : (a + 1) * n_row, j]
                if chunk == 0
                else in_b[a * n_row : (a + 1) * n_row, j, t]
            ).reshape(n_row * 16, 128)
            for a in range(n_ma)
            for t in range(tiles)
        ]
        parts = curl(rows, (legendre[j], shared[j]), upper, horizontal, matrices)
        for (part, c), values in parts.items():
            (current_ref, vorticity_ref)[chunk][part, c, j] = values

    for t in range(tiles):
        all_a(t, recv_a.at[t])
    for copy in copy_own(0):
        copy.wait()

    def first(j, _):
        transform(0, j)
        return 0

    lax.fori_loop(0, slots, first, 0)
    for copy in copy_own(1):
        copy.wait()
    for t in range(tiles):
        all_a(t, send_a.at[t])
    for g in range(len(groups)):
        if g > 0:
            all_b(g - 1, send_b.at[g - 1])
        all_b(g, recv_b.at[g])

        def second(k, _):
            transform(1, groups[g][0] + k)
            return 0

        if g < len(groups) - 1:
            lax.fori_loop(0, groups[g][1], second, 0)
        if g == 0:
            for copy in last_copies:
                copy.wait()
    all_b(len(groups) - 1, send_b.at[len(groups) - 1])


def write_kernel(
    current, vorticity, last_in, last_tables, last_rows, matrices, current_hbm, vorticity_hbm,
    staged, sem, last_sem,
):
    last = vorticity.shape[2] - 1
    copies = []
    for part in range(3):
        for c in (0, 1):
            copies.append(
                pltpu.make_async_copy(
                    vorticity.at[part, c, pl.ds(0, last)],
                    vorticity_hbm.at[part, c, pl.ds(0, last)],
                    sem.at[0, part, c],
                )
            )
            copies.append(
                pltpu.make_async_copy(
                    current.at[part, c], current_hbm.at[part, c], sem.at[1, part, c]
                )
            )
    for copy in copies:
        copy.start()
    bands, count = 4, last_in.shape[0] // 4
    rows = [
        last_in[a * count : (a + 1) * count, t].reshape(count * 16, 128)
        for a in range(bands)
        for t in range(last_in.shape[1])
    ]
    width = staged.shape[3] // 2
    for h in (0, 1):
        columns = slice(h * width, (h + 1) * width)
        parts = curl(
            rows,
            (last_tables[0, :, columns], last_tables[1, :, columns]),
            last_rows[0, :, columns].astype(jnp.int32),
            last_rows[1, :, columns],
            matrices,
        )
        for (part, c), values in parts.items():
            staged[part, c, :, columns] = values
            copy = pltpu.make_async_copy(
                staged.at[part, c, :, columns],
                vorticity_hbm.at[part, c, last, :, columns],
                last_sem.at[h, part, c],
            )
            copy.start()
            copies.append(copy)
    for copy in copies:
        copy.wait()


def kernel_shards(
    grid_fields, pair_list, legendre, stencil_start, first_weights, second_weights, inv_radius
):
    _, _, lat, points = grid_fields.shape
    slots, depth, degrees = legendre.shape
    n_ma, n_row = lax.axis_size("ma"), lax.axis_size("row")
    devices = n_ma * n_row
    pairs = pair_list.shape[0]
    radii = 2 * n_row
    tiles = lat // 128
    half = points // 2
    groups = [(0, slots - 1), (slots - 1, 1)]
    table = jnp.asarray(order_table(pairs, degrees, points))
    out_dims = (3, 2, slots, radii, degrees)
    anywhere = pl.BlockSpec(memory_space=pl.ANY)
    dims = (n_ma, n_row, slots, lat, half, degrees, pairs, groups)
    macs = 8 * lat * half * pairs * 4 + 2 * slots * 128 * 2 * depth * degrees
    held = (
        pltpu.VMEM(out_dims, BF16),
        pltpu.VMEM(out_dims, BF16),
        pltpu.VMEM((devices, tiles, 16, 128), BF16),
        pltpu.VMEM((2, depth, degrees), BF16),
        pltpu.VMEM((2, 1, degrees), F32),
        pltpu.VMEM((2, 8 * radii, 8 * radii), BF16),
    )
    results = pl.pallas_call(
        functools.partial(kernel, dims),
        out_shape=held,
        in_specs=[pl.BlockSpec(memory_space=pltpu.SMEM)] * 3
        + [pl.BlockSpec(memory_space=pltpu.VMEM)]
        + [anywhere] * 5,
        out_specs=(pl.BlockSpec(memory_space=pltpu.VMEM),) * len(held),
        scratch_shapes=[
            pltpu.VMEM(first_weights.shape[::-1], F32),
            pltpu.VMEM(second_weights.shape[::-1], F32),
            pltpu.VMEM(table.shape, BF16),
            pltpu.VMEM((slots, depth, degrees), BF16),
            pltpu.VMEM((8, 2 * lat, half), BF16),
            pltpu.VMEM((2, 512, half), BF16),
            pltpu.VMEM((pairs, pairs), BF16),
            pltpu.VMEM((512, 4 * pairs), BF16),
            pltpu.VMEM((pairs * 16, 128), F32),
            pltpu.VMEM((tiles, devices, slots, 16, 128), BF16),
            pltpu.VMEM((devices, slots, tiles, 16, 128), BF16),
            pltpu.VMEM((tiles, devices, slots, 16, 128), BF16),
            pltpu.VMEM((devices, slots - 1, tiles, 16, 128), BF16),
            pltpu.SemaphoreType.DMA((2,)),
            pltpu.SemaphoreType.DMA((4, 2, tiles, 2)),
            pltpu.SemaphoreType.DMA((2,)),
            pltpu.SemaphoreType.DMA((slots,)),
            pltpu.SemaphoreType.DMA((3,)),
            pltpu.SemaphoreType.DMA((2,)),
            pltpu.SemaphoreType.DMA((tiles,)),
            pltpu.SemaphoreType.DMA((tiles,)),
            pltpu.SemaphoreType.DMA((len(groups),)),
            pltpu.SemaphoreType.DMA((len(groups),)),
        ],
        compiler_params=pltpu.CompilerParams(
            collective_id=0, has_side_effects=True, vmem_limit_bytes=50 * 2**20
        ),
        cost_estimate=pl.CostEstimate(
            flops=2 * macs, bytes_accessed=2 * (grid_fields.size + legendre.size), transcendentals=0
        ),
    )(
        pair_list,
        stencil_start,
        inv_radius,
        pair_list.reshape(1, pairs),
        first_weights.T,
        second_weights.T,
        grid_fields,
        table,
        legendre,
    )
    out = jax.ShapeDtypeStruct(out_dims, BF16)
    return pl.pallas_call(
        write_kernel,
        out_shape=(out, out),
        in_specs=[pl.BlockSpec(memory_space=pltpu.VMEM)] * len(held),
        out_specs=(anywhere, anywhere),
        scratch_shapes=[
            pltpu.VMEM((3, 2, radii, degrees), BF16),
            pltpu.SemaphoreType.DMA((2, 3, 2)),
            pltpu.SemaphoreType.DMA((2, 3, 2)),
        ],
        compiler_params=pltpu.CompilerParams(vmem_limit_bytes=16 * 2**20),
    )(*[pltpu.with_memory_space_constraint(part, pltpu.VMEM) for part in results])


def solution(mesh):
    in_specs = (P(None, "row", "ma", None), P(), P(("ma", "row"), None, None), P(), P(), P(), P())
    out_specs = (P(None, None, ("ma", "row"), None, None), P(None, None, ("ma", "row"), None, None))
    n_ma, n_row = mesh.shape["ma"], mesh.shape["row"]

    def shards(*args):
        potentials, rad_local, lat, points = args[0].shape
        slots, depth, degrees = args[2].shape
        fits = (
            potentials == 4
            and rad_local == 2
            and lat % 128 == 0
            and depth % 256 == 0
            and degrees % 128 == 0
            and points % 1024 == 0
            and slots == 8
            and n_ma == 4
            and n_row == 8
            and args[1].shape[0] == 256
            and depth == 2 * lat
            and degrees == points // 2
        )
        return (kernel_shards if fits else plain_shards)(*args)

    return jax.shard_map(shards, mesh=mesh, in_specs=in_specs, out_specs=out_specs, check_vma=False)
```
